32 devices in a mesh: star: 8 (over y, x, core), row: 4 (over z).
Axes of the slice: x: 2, y: 2, z: 4, core: 2. Of those that a mesh axis runs over, the one named last changes fastest.
Arguments:
- feature_maps: bfloat16 [64, 1024, 1024], P(None, 'row'), may hold values from -6 to 6
- coef_table: bfloat16 [64, 64], replicated, may hold values from -0.119628906 to 0.119628906
- star_counts: int32 [8], replicated, may hold values from 1 to 12, 32 in all
- star_cells: int32 [8, 12], replicated, may hold values from 0 to 63
- star_bands: int32 [8, 12], replicated, may hold values from 0 to 7
- psf_cotangent: bfloat16 [96, 1024, 1024], P('star', 'row'), may hold values from -6 to 6
Outputs:
- map_grad: float32 [64, 1024, 1024], P('star', 'row')
- coef_grad: float32 [64, 64], replicated
The draws below stay inside these ranges and needn't reach their ends.
Inputs may be any that keep to these rules, and one draw needn't show every extreme that they name: The live stars of group g fill its slots 0 to star_counts[g] - 1; the counts sum to 32, and some group has exactly 12.
All inputs are finite; a program needn't handle non-finite values.
Results may differ from the reference program's by a relative error of at most 0.008.
Values may be sent and summed in bfloat16 or wider, within the bound.
A program may use at most 192 MiB of HBM per device.

```python
import math
import jax
import jax.numpy as jnp
import numpy as np
from jax import lax

PUPIL = 1024
MAPS = 64
CELLS = 64
BANDS = 8
SLOT = 12
TOTAL = 32
N_STAR = 8


def spread_values(key, limit, length):
    first_key, second_key = jax.random.split(key)
    values = jax.random.randint(first_key, (length,), 0, limit, dtype=jnp.int32)
    places = jax.random.permutation(second_key, length)
    values = values.at[places[0]].set(limit - 1)
    return values.at[places[1]].set(0)


def draw_star_cells(key, part):
    return spread_values(jax.random.fold_in(key, 11), CELLS, N_STAR * SLOT).reshape(N_STAR, SLOT)


def draw_star_bands(key, part):
    return spread_values(jax.random.fold_in(key, 23), BANDS, N_STAR * SLOT).reshape(N_STAR, SLOT)


def steps_of(stream_key, extent, shards, smallest, largest):
    def one(axis_at, blocks):
        draws = jax.random.uniform(jax.random.fold_in(jax.random.fold_in(stream_key, 6), axis_at), (blocks,), jnp.float32, smallest / len(shards), largest / len(shards))
        return jnp.repeat(jnp.exp(draws), extent[axis_at] // blocks).reshape((-1,) + (1,) * (len(extent) - axis_at - 1))

    factor_of = one(*shards[0])
    for cut in shards[1:]:
        factor_of = factor_of * one(*cut)
    return factor_of


def split_up(number_of, total, most, lean):
    loads = [(1 << 20) // math.isqrt(rank ** lean) + 1 for rank in range(2, number_of + 1)]
    spare, holding = total - most - (number_of - 1), [1] * (number_of - 1)
    while spare > 0:
        free = [i for i in range(number_of - 1) if holding[i] < most]
        mass, budget = sum([loads[i] for i in free]), spare
        for i in free:
            more = min(most - holding[i], max(1, budget * loads[i] // mass), spare)
            holding[i] = holding[i] + more
            spare = spare - more
    return np.array([most] + holding)


def uneven_parts(rng, number_of, total, bound, slope):
    if number_of == 2:
        one = jax.random.randint(rng, (), max(1, total - bound), min(bound, total - 1) + 1)
        return jnp.stack([one, total - one])
    sizes = jnp.asarray(split_up(number_of, total, bound, slope), jnp.int32)
    twos = (number_of - 1) // 2
    donor, sink = sizes[1:1 + 2 * twos:2], sizes[2:2 + 2 * twos:2]
    slack = jnp.minimum(donor - 1, bound - sink)
    passed = jax.random.randint(jax.random.fold_in(rng, 1), (twos,), 0, 1 << 20) % (slack + 1)
    sizes = sizes.at[1:1 + 2 * twos:2].set(donor - passed).at[2:2 + 2 * twos:2].set(sink + passed)
    return sizes[jax.random.permutation(jax.random.fold_in(rng, 2), number_of)]


def noise(key, extent, scale, bound, shards=(), kind=jnp.bfloat16):
    level = steps_of(key, extent, shards, -0.22, 0.18) if shards else 1.0
    result = jax.random.normal(key, extent, jnp.float32) * scale * level
    return jnp.minimum(jnp.maximum(result, -bound), bound).astype(kind)


def setup_inputs(seed: int = 0) -> dict:
    key_of = jax.random.split(jax.random.key(seed), 7)
    feature_maps = noise(key_of[0], (MAPS, PUPIL, PUPIL), 1.0, 6.0, ((1, 4),))
    coef_table = noise(key_of[1], (CELLS, MAPS), 0.02, 0.119628906)
    star_counts = uneven_parts(key_of[2], N_STAR, TOTAL, SLOT, 2).astype(jnp.int32)
    star_cells = draw_star_cells(jax.random.fold_in(key_of[6], 71), 0)
    star_bands = draw_star_bands(jax.random.fold_in(key_of[6], 71), 0)
    psf_cotangent = noise(key_of[5], (N_STAR * SLOT, PUPIL, PUPIL), 1.0, 6.0, ((0, 8), (1, 4)))
    return {"feature_maps": feature_maps, "coef_table": coef_table, "star_counts": star_counts, "star_cells": star_cells, "star_bands": star_bands, "psf_cotangent": psf_cotangent}


def fourier_tables(pupil_size):
    index_row = jnp.arange(pupil_size, dtype=jnp.int32)
    products = (index_row[:, None] * index_row[None, :]) % pupil_size
    angles = (2.0 * jnp.pi / pupil_size) * products.astype(jnp.float32)
    return jnp.cos(angles).astype(jnp.bfloat16), (-jnp.sin(angles)).astype(jnp.bfloat16)


def aperture_rows(first_row, row_count, pupil_size):
    centre = 0.5 * (pupil_size - 1)
    row_pos = (first_row + jnp.arange(row_count, dtype=jnp.int32)).astype(jnp.float32) - centre
    col_pos = jnp.arange(pupil_size, dtype=jnp.int32).astype(jnp.float32) - centre
    radius = row_pos[:, None] * row_pos[:, None] + col_pos[None, :] * col_pos[None, :]
    return jnp.where(radius <= 0.25 * pupil_size * pupil_size, 1.0, 0.0).astype(jnp.float32)


def wave_numbers(band_ids):
    wavelength = 0.55 + 0.35 * band_ids.astype(jnp.float32) / (BANDS - 1)
    return 2.0 * jnp.pi / wavelength


def product(left, right):
    return jnp.dot(left.astype(jnp.float32), right.astype(jnp.float32), precision=lax.Precision.HIGHEST)


def star_gradient(flat_maps, coef_row, band_id, cotangent, cos_table, sin_table, aperture):
    pupil_size = aperture.shape[0]
    path_error = product(coef_row[None, :], flat_maps)[0].reshape(pupil_size, pupil_size)
    wave_number = wave_numbers(band_id)
    phase_angle = wave_number * path_error
    cos_phase = jnp.cos(phase_angle)
    sin_phase = jnp.sin(phase_angle)
    pupil_real = (aperture * cos_phase).astype(jnp.bfloat16)
    pupil_imag = (aperture * sin_phase).astype(jnp.bfloat16)
    column_real = (product(pupil_real, cos_table) - product(pupil_imag, sin_table)).astype(jnp.bfloat16)
    column_imag = (product(pupil_real, sin_table) + product(pupil_imag, cos_table)).astype(jnp.bfloat16)
    inverse = 1.0 / pupil_size
    focal_real = (product(column_real.T, cos_table) - product(column_imag.T, sin_table)) * inverse
    focal_imag = (product(column_real.T, sin_table) + product(column_imag.T, cos_table)) * inverse
    grad_real = (2.0 * cotangent * focal_real).astype(jnp.bfloat16)
    grad_imag = (2.0 * cotangent * focal_imag).astype(jnp.bfloat16)
    back_real = ((product(grad_real, cos_table) + product(grad_imag, sin_table)) * inverse).astype(jnp.bfloat16)
    back_imag = ((product(grad_imag, cos_table) - product(grad_real, sin_table)) * inverse).astype(jnp.bfloat16)
    pupil_greal = product(back_real.T, cos_table) + product(back_imag.T, sin_table)
    pupil_gimag = product(back_imag.T, cos_table) - product(back_real.T, sin_table)
    phase_grad = aperture * (cos_phase * pupil_gimag - sin_phase * pupil_greal)
    return (wave_number * phase_grad).astype(jnp.bfloat16)


def reference(feature_maps, coef_table, star_counts, star_cells, star_bands, psf_cotangent):
    map_count = feature_maps.shape[0]
    pupil_size = feature_maps.shape[1]
    slot_count = star_cells.shape[1]
    flat_maps = feature_maps.reshape(map_count, pupil_size * pupil_size).astype(jnp.float32)
    cos_table, sin_table = fourier_tables(pupil_size)
    aperture = aperture_rows(0, pupil_size, pupil_size)
    group_ends = jnp.cumsum(star_counts).astype(jnp.int32)
    group_starts = (group_ends - star_counts).astype(jnp.int32)
    flat_cells = star_cells.reshape(-1)
    flat_bands = star_bands.reshape(-1)

    def star_step(running, star_rank):
        map_total, coef_total = running
        owner_group = jnp.sum((group_ends <= star_rank).astype(jnp.int32)).astype(jnp.int32)
        slot_index = (owner_group * slot_count + star_rank - group_starts[owner_group]).astype(jnp.int32)
        cell_id = flat_cells[slot_index]
        band_id = flat_bands[slot_index]
        coef_row = coef_table[cell_id].astype(jnp.float32)
        cotangent = lax.dynamic_index_in_dim(psf_cotangent, slot_index, 0, keepdims=False).astype(jnp.float32)
        path_grad = star_gradient(flat_maps, coef_row, band_id, cotangent, cos_table, sin_table, aperture)
        flat_grad = path_grad.reshape(1, pupil_size * pupil_size).astype(jnp.float32)
        map_total = map_total + product(coef_row[:, None], flat_grad)
        map_scores = product(flat_maps, flat_grad.T)[:, 0] / (8 * pupil_size)
        coef_total = coef_total.at[cell_id].add(map_scores)
        return (map_total, coef_total), jnp.zeros((), jnp.float32)

    initial = (jnp.zeros((map_count, pupil_size * pupil_size), jnp.float32), jnp.zeros(coef_table.shape, jnp.float32))
    finished, unused = lax.scan(star_step, initial, jnp.arange(TOTAL, dtype=jnp.int32))
    return finished[0].reshape(map_count, pupil_size, pupil_size), finished[1]
```

```python
import functools

import jax
import jax.numpy as jnp
import numpy as np
from jax import lax
from jax.experimental import pallas as pl
from jax.experimental.pallas import tpu as pltpu
from jax.sharding import PartitionSpec as P

BANDS = 8
LIVE_DEV = 4
RADIX = 4
ROWS_STEP = 16
F32 = jnp.float32
BF16 = jnp.bfloat16


def fourier_tables(pupil_size):
    index_row = jnp.arange(pupil_size, dtype=jnp.int32)
    products = index_row[:, None] * index_row[None, :] % pupil_size
    angles = 2.0 * jnp.pi / pupil_size * products.astype(jnp.float32)
    return (jnp.cos(angles).astype(jnp.bfloat16), (-jnp.sin(angles)).astype(jnp.bfloat16))


def aperture_rows(first_row, row_count, pupil_size):
    centre = 0.5 * (pupil_size - 1)
    row_pos = (first_row + jnp.arange(row_count, dtype=jnp.int32)).astype(jnp.float32) - centre
    col_pos = jnp.arange(pupil_size, dtype=jnp.int32).astype(jnp.float32) - centre
    radius = row_pos[:, None] * row_pos[:, None] + col_pos[None, :] * col_pos[None, :]
    return jnp.where(radius <= 0.25 * pupil_size * pupil_size, 1.0, 0.0).astype(jnp.float32)


def wave_numbers(band_ids):
    wavelength = 0.55 + 0.35 * band_ids.astype(jnp.float32) / (BANDS - 1)
    return 2.0 * jnp.pi / wavelength


def table_pick(values, indices):
    positions = jnp.arange(values.shape[0], dtype=jnp.int32)
    chosen = jnp.where(positions[None, :] == indices[:, None], values[None, :], 0)
    return jnp.sum(chosen, axis=1)


def per_device(feature_maps, coef_table, star_counts, star_cells, star_bands, psf_cotangent):
    groups = lax.axis_size("star")
    my_group = lax.axis_index("star")
    slot_count = psf_cotangent.shape[0]
    map_count, row_count, pupil_size = feature_maps.shape
    group_ends = jnp.cumsum(star_counts)
    group_starts = group_ends - star_counts
    flat_cells = star_cells.reshape(-1)
    flat_bands = star_bands.reshape(-1)
    cell_count = coef_table.shape[0]
    capacity = -(-slot_count // groups)
    targets = jnp.arange(groups, dtype=jnp.int32)
    lane_index = jnp.arange(capacity, dtype=jnp.int32)
    my_start = table_pick(group_starts, my_group[None])
    my_count = table_pick(star_counts, my_group[None])
    first_slot = (targets - my_start) % groups
    send_slot = (first_slot[:, None] + lane_index[None, :] * groups).reshape(-1)
    valid_mask = send_slot < my_count
    picked = jnp.take(psf_cotangent, jnp.minimum(send_slot, slot_count - 1), axis=0)
    outgoing = jnp.where(valid_mask[:, None, None], picked, jnp.zeros_like(picked))
    incoming = lax.all_to_all(outgoing, "star", split_axis=0, concat_axis=0, tiled=True)
    star_rank = my_group + jnp.arange(LIVE_DEV, dtype=jnp.int32) * groups
    owner_group = jnp.sum((group_ends[None, :] <= star_rank[:, None]).astype(jnp.int32), axis=1)
    within = star_rank - table_pick(group_starts, owner_group)
    live_mask = jnp.ones((LIVE_DEV,), dtype=bool)
    owner_group, within, live_mask = (owner_group, within, live_mask)
    cotangent = jnp.take(incoming, owner_group * capacity + within // groups, axis=0)
    slot_index = owner_group * slot_count + within
    cell_ids = table_pick(flat_cells, slot_index)
    band_ids = table_pick(flat_bands, slot_index)
    cell_hot = cell_ids[:, None] == jnp.arange(cell_count, dtype=jnp.int32)[None, :]
    coef_rows = jnp.dot(
        cell_hot.astype(jnp.bfloat16), coef_table, preferred_element_type=jnp.float32
    ).astype(jnp.bfloat16)
    flat_maps = feature_maps.reshape(map_count, row_count * pupil_size)
    path_error = jnp.dot(coef_rows, flat_maps, preferred_element_type=jnp.float32).reshape(
        -1, row_count, pupil_size
    )
    wave_number = wave_numbers(band_ids)
    phase_angle = wave_number[:, None, None] * path_error
    aperture = aperture_rows(lax.axis_index("row") * row_count, row_count, pupil_size)
    cos_phase = jnp.cos(phase_angle)
    sin_phase = jnp.sin(phase_angle)
    pupil_field = jnp.stack([aperture * cos_phase, aperture * sin_phase], 1).astype(jnp.bfloat16)
    cos_table, sin_table = fourier_tables(pupil_size)
    inverse = 1.0 / pupil_size
    along_cos = jnp.einsum(
        "sarc,cv->sarv", pupil_field, cos_table, preferred_element_type=jnp.float32
    )
    along_sin = jnp.einsum(
        "sarc,cv->sarv", pupil_field, sin_table, preferred_element_type=jnp.float32
    )
    column_field = jnp.stack(
        [along_cos[:, 0] - along_sin[:, 1], along_sin[:, 0] + along_cos[:, 1]], 1
    ).astype(jnp.bfloat16)
    pieces = lax.all_to_all(column_field, "row", split_axis=3, concat_axis=2, tiled=True)
    row_cos = jnp.einsum("sarv,ru->savu", pieces, cos_table, preferred_element_type=jnp.float32)
    row_sin = jnp.einsum("sarv,ru->savu", pieces, sin_table, preferred_element_type=jnp.float32)
    real_part = (row_cos[:, 0] - row_sin[:, 1]) * inverse
    imag_part = (row_sin[:, 0] + row_cos[:, 1]) * inverse
    focal_field = jnp.stack([real_part, imag_part], 1)
    weight = jnp.where(live_mask, 2.0, 0.0).astype(jnp.float32)[:, None, None, None]
    focal_grad = (weight * cotangent.astype(jnp.float32)[:, None] * focal_field).astype(
        jnp.bfloat16
    )
    back_cos = jnp.einsum(
        "savu,ur->savr", focal_grad, cos_table, preferred_element_type=jnp.float32
    )
    back_sin = jnp.einsum(
        "savu,ur->savr", focal_grad, sin_table, preferred_element_type=jnp.float32
    )
    spectrum_grad = jnp.stack(
        [(back_cos[:, 0] + back_sin[:, 1]) * inverse, (back_cos[:, 1] - back_sin[:, 0]) * inverse],
        1,
    ).astype(jnp.bfloat16)
    pieces = lax.all_to_all(spectrum_grad, "row", split_axis=3, concat_axis=2, tiled=True)
    col_cos = jnp.einsum("savr,vc->sarc", pieces, cos_table, preferred_element_type=jnp.float32)
    col_sin = jnp.einsum("savr,vc->sarc", pieces, sin_table, preferred_element_type=jnp.float32)
    pupil_grad = jnp.stack([col_cos[:, 0] + col_sin[:, 1], col_cos[:, 1] - col_sin[:, 0]], 1)
    phase_grad = aperture * (cos_phase * pupil_grad[:, 1] - sin_phase * pupil_grad[:, 0])
    path_grad = (
        (wave_number[:, None, None] * phase_grad)
        .astype(jnp.bfloat16)
        .reshape(-1, row_count * pupil_size)
    )
    map_scores = lax.dot_general(
        path_grad, flat_maps, (((1,), (1,)), ((), ())), preferred_element_type=jnp.float32
    )
    coef_part = lax.dot_general(
        cell_hot.astype(jnp.float32),
        map_scores * (1.0 / (8 * pupil_size)),
        (((0,), (0,)), ((), ())),
        precision=lax.Precision.HIGHEST,
    )
    coef_grad = lax.psum(coef_part, ("star", "row"))
    share = map_count // groups
    map_grad = lax.psum_scatter(
        lax.dot_general(
            coef_rows, path_grad, (((0,), (0,)), ((), ())), preferred_element_type=jnp.float32
        ),
        "star",
        scatter_dimension=0,
        tiled=True,
    )
    return (map_grad.reshape(share, row_count, pupil_size), coef_grad)


def quarter_tables(size):
    quarter = size // RADIX
    place = np.arange(quarter)[None, :, None]
    freq = RADIX * np.arange(quarter)[None, None, :] + np.arange(RADIX)[:, None, None]
    angle = 2.0 * np.pi / size * ((place * freq) % size)
    cosine, sine = np.cos(angle), -np.sin(angle)
    right = np.concatenate(
        [np.concatenate([cosine, sine], 2), np.concatenate([-sine, cosine], 2)], 1
    ).astype(np.float32)
    left = np.swapaxes(right, 1, 2)
    return jnp.asarray(right.astype(jnp.bfloat16)), jnp.asarray(left.astype(jnp.bfloat16))


def turn_cos_sin(turns):
    half = turns * np.float32(np.pi)
    square = half * half
    sine = jnp.full_like(square, -1.0 / 39916800.0)
    for term in (1.0 / 362880.0, -1.0 / 5040.0, 1.0 / 120.0, -1.0 / 6.0, 1.0):
        sine = sine * square + np.float32(term)
    sine = sine * half
    cosine = jnp.full_like(square, 1.0 / 479001600.0)
    for term in (-1.0 / 3628800.0, 1.0 / 40320.0, -1.0 / 720.0, 1.0 / 24.0, -0.5, 1.0):
        cosine = cosine * square + np.float32(term)
    return 1.0 - 2.0 * sine * sine, 2.0 * sine * cosine


def butterfly(real, imag, sign):
    sr, dr = real[0] + real[2], real[0] - real[2]
    si, di = imag[0] + imag[2], imag[0] - imag[2]
    tr, er = real[1] + real[3], real[1] - real[3]
    ti, ei = imag[1] + imag[3], imag[1] - imag[3]
    if sign < 0:
        er, ei = -er, -ei
    return (
        [sr + tr, dr - ei, sr - tr, dr + ei],
        [si + ti, di + er, si - ti, di - er],
    )


def phase_kernel(inverse_ref, weight_ref, maps_ref, out_ref):
    stars, rows, size = out_ref.shape
    maps = maps_ref[...].reshape(maps_ref.shape[0] * rows, size)
    path = jnp.dot(weight_ref[...], maps, preferred_element_type=F32)
    for star in range(stars):
        turns = path[star * rows : (star + 1) * rows] * inverse_ref[star]
        out_ref[star] = (turns - jnp.floor(turns + 0.5)).astype(BF16)


def phase_turns(inverse_wave, coef_rows, feature_maps):
    map_count, row_count, size = feature_maps.shape
    stars = coef_rows.shape[0]
    weights = spread_rows(coef_rows)
    return pl.pallas_call(
        phase_kernel,
        out_shape=jax.ShapeDtypeStruct((stars, row_count, size), BF16),
        grid=(row_count // ROWS_STEP,),
        in_specs=[
            pl.BlockSpec(memory_space=pltpu.SMEM),
            pl.BlockSpec(weights.shape, lambda i: (0, 0)),
            pl.BlockSpec((map_count, ROWS_STEP, size), lambda i: (0, i, 0)),
        ],
        out_specs=pl.BlockSpec((stars, ROWS_STEP, size), lambda i: (0, i, 0)),
        cost_estimate=pl.CostEstimate(
            flops=2 * stars * ROWS_STEP * map_count * row_count * size,
            bytes_accessed=2 * (map_count + stars) * row_count * size,
            transcendentals=0,
        ),
        compiler_params=pltpu.CompilerParams(vmem_limit_bytes=24 << 20),
        name="phase_turns",
    )(inverse_wave, weights, feature_maps)


def spread_rows(weights):
    eye = jnp.eye(ROWS_STEP, dtype=weights.dtype)
    outs, ins = weights.shape
    spread = weights[:, None, :, None] * eye[None, :, None, :]
    return spread.reshape(outs * ROWS_STEP, ins * ROWS_STEP)


def star_kernel(
    chunk, wave_ref, turns_ref, cot_ref, right_ref, left_ref, out_ref, pr, pi, yr, yi, ct, xr, xi
):
    size = turns_ref.shape[1]
    quarter = size // RADIX
    steps = size // chunk
    blocks = [slice(m * quarter, (m + 1) * quarter) for m in range(RADIX)]
    centre = 0.5 * (size - 1)
    scale = 1.0 / size

    def forward_columns(step, carry):
        rows = pl.ds(pl.multiple_of(step * chunk, chunk), chunk)
        cosine, sine = turn_cos_sin(turns_ref[rows, :].astype(F32))
        row_pos = (
            lax.broadcasted_iota(jnp.int32, (chunk, size), 0) + step * chunk
        ).astype(F32) - centre
        col_pos = lax.broadcasted_iota(jnp.int32, (chunk, size), 1).astype(F32) - centre
        inside = row_pos * row_pos + col_pos * col_pos <= 0.25 * size * size
        real = jnp.where(inside, cosine, 0.0)
        imag = jnp.where(inside, sine, 0.0)
        pr[rows, :] = real
        pi[rows, :] = imag
        mixed_real, mixed_imag = butterfly(
            [real[:, b] for b in blocks], [imag[:, b] for b in blocks], -1
        )
        for k in range(RADIX):
            both = jnp.concatenate([mixed_real[k].astype(BF16), mixed_imag[k].astype(BF16)], 1)
            made = jnp.dot(both, right_ref[k], preferred_element_type=F32).astype(BF16)
            yr[rows, blocks[k]] = made[:, :quarter]
            yi[rows, blocks[k]] = made[:, quarter:]
        return carry

    lax.fori_loop(0, steps, forward_columns, 0)

    def pick(k):
        j = lax.broadcasted_iota(jnp.int32, (quarter, size), 0)
        f = lax.broadcasted_iota(jnp.int32, (quarter, size), 1)
        return jnp.where(f == RADIX * j + k, 1.0, 0.0).astype(BF16)

    nt = (((1,), (1,)), ((), ()))
    for k in range(RADIX):
        part = lax.dot_general(
            pick(k), cot_ref[...], nt, preferred_element_type=F32
        ).astype(BF16)
        for m in range(RADIX):
            ct[blocks[k], blocks[m]] = lax.dot_general(
                part, pick(m), nt, preferred_element_type=F32
            )

    def focal(step, carry):
        cols = pl.ds(pl.multiple_of(step * quarter, quarter), quarter)
        mixed_real, mixed_imag = butterfly(
            [yr[b, cols].astype(F32) for b in blocks],
            [yi[b, cols].astype(F32) for b in blocks],
            -1,
        )
        back_real, back_imag = [], []
        for k in range(RADIX):
            both = jnp.concatenate([mixed_real[k].astype(BF16), mixed_imag[k].astype(BF16)], 0)
            field = jnp.dot(left_ref[k], both, preferred_element_type=F32)
            weight = ct[blocks[k], cols] * (2.0 * scale)
            grad = (field * jnp.concatenate([weight, weight], 0)).astype(BF16)
            back = jnp.dot(right_ref[k], grad, preferred_element_type=F32)
            back_real.append(back[:quarter])
            back_imag.append(back[quarter:])
        spec_real, spec_imag = butterfly(back_real, back_imag, 1)
        for m in range(RADIX):
            xr[blocks[m], cols] = (spec_real[m] * scale).astype(BF16)
            xi[blocks[m], cols] = (spec_imag[m] * scale).astype(BF16)
        return carry

    lax.fori_loop(0, RADIX, focal, 0)

    def inverse_columns(step, carry):
        rows = pl.ds(pl.multiple_of(step * chunk, chunk), chunk)
        part_real, part_imag = [], []
        for k in range(RADIX):
            both = jnp.concatenate([xr[rows, blocks[k]], xi[rows, blocks[k]]], 1)
            made = jnp.dot(both, left_ref[k], preferred_element_type=F32)
            part_real.append(made[:, :quarter])
            part_imag.append(made[:, quarter:])
        grad_real, grad_imag = butterfly(part_real, part_imag, 1)
        wave = wave_ref[0]
        for m in range(RADIX):
            grad = pr[rows, blocks[m]] * grad_imag[m] - pi[rows, blocks[m]] * grad_real[m]
            out_ref[rows, blocks[m]] = (wave * grad).astype(BF16)
        return carry

    lax.fori_loop(0, steps, inverse_columns, 0)


def star_gradient(wave, turns, cotangent, right, left):
    size = turns.shape[0]
    vmem = pl.BlockSpec(memory_space=pltpu.VMEM)
    square = (size, size)
    return pl.pallas_call(
        functools.partial(star_kernel, 128),
        out_shape=jax.ShapeDtypeStruct(square, BF16),
        in_specs=[pl.BlockSpec(memory_space=pltpu.SMEM), vmem, vmem, vmem, vmem],
        out_specs=vmem,
        scratch_shapes=[
            pltpu.VMEM(square, F32),
            pltpu.VMEM(square, F32),
            pltpu.VMEM(square, BF16),
            pltpu.VMEM(square, BF16),
            pltpu.VMEM(square, F32),
            pltpu.VMEM(square, BF16),
            pltpu.VMEM(square, BF16),
        ],
        compiler_params=pltpu.CompilerParams(vmem_limit_bytes=56 << 20),
        name="star_gradient",
    )(wave, turns, cotangent, right, left)


def maps_kernel(group_ref, weight_ref, grad_ref, maps_ref, out_ref, score_ref):
    share, rows, size = out_ref.shape
    grads = grad_ref[...].reshape(grad_ref.shape[0] * rows, size)
    maps = maps_ref[...].reshape(share * rows, size)
    total = jnp.dot(weight_ref[...], grads, preferred_element_type=F32)
    out_ref[...] = total.reshape(share, rows, size)

    @pl.when(pl.program_id(0) == 0)
    def _():
        score_ref[...] = jnp.zeros_like(score_ref)

    score_ref[...] += lax.dot_general(
        maps, grads, (((1,), (1,)), ((), ())), preferred_element_type=F32
    )


def map_sums(my_group, coef_rows, path_grads, feature_maps, share):
    stars, row_count, size = path_grads.shape
    weights = spread_rows(coef_rows)
    score_shape = (share * ROWS_STEP, stars * ROWS_STEP)
    map_grad, scores = pl.pallas_call(
        maps_kernel,
        out_shape=(
            jax.ShapeDtypeStruct((share, row_count, size), F32),
            jax.ShapeDtypeStruct(score_shape, F32),
        ),
        grid_spec=pltpu.PrefetchScalarGridSpec(
            num_scalar_prefetch=1,
            grid=(row_count // ROWS_STEP,),
            in_specs=[
                pl.BlockSpec(weights.shape, lambda i, g: (0, 0)),
                pl.BlockSpec((stars, ROWS_STEP, size), lambda i, g: (0, i, 0)),
                pl.BlockSpec((share, ROWS_STEP, size), lambda i, g: (g[0], i, 0)),
            ],
            out_specs=(
                pl.BlockSpec((share, ROWS_STEP, size), lambda i, g: (0, i, 0)),
                pl.BlockSpec(score_shape, lambda i, g: (0, 0)),
            ),
        ),
        compiler_params=pltpu.CompilerParams(vmem_limit_bytes=24 << 20),
        name="map_sums",
    )(my_group[None], weights, path_grads, feature_maps)
    eye = jnp.eye(ROWS_STEP, dtype=F32)
    scores = scores.reshape(share, ROWS_STEP, stars, ROWS_STEP)
    return map_grad, jnp.sum(scores * eye[None, :, None, :], axis=(1, 3))


def star_devices(feature_maps, coef_table, star_counts, star_cells, star_bands, psf_cotangent):
    groups = lax.axis_size("star")
    lanes = lax.axis_size("row")
    my_group = lax.axis_index("star")
    my_lane = lax.axis_index("row")
    slot_count = psf_cotangent.shape[0]
    map_count, row_count, size = feature_maps.shape
    cell_count = coef_table.shape[0]
    share = map_count // groups
    group_ends = jnp.cumsum(star_counts)
    group_starts = group_ends - star_counts
    capacity = -(-slot_count // groups)
    targets = jnp.arange(groups, dtype=jnp.int32)
    my_start = table_pick(group_starts, my_group[None])
    first_slot = (targets - my_start) % groups
    lane_index = jnp.arange(capacity, dtype=jnp.int32)
    send_slot = (first_slot[:, None] + lane_index[None, :] * groups).reshape(-1)
    outgoing = jnp.take(
        psf_cotangent, jnp.minimum(send_slot, slot_count - 1), axis=0, mode="clip"
    )
    incoming = lax.all_to_all(outgoing, "star", split_axis=0, concat_axis=0, tiled=True)

    total = groups * lanes
    order = jnp.arange(total, dtype=jnp.int32)
    rank = order // lanes + (order % lanes) * groups
    owner = jnp.sum((group_ends[None, :] <= rank[:, None]).astype(jnp.int32), axis=1)
    within = rank - table_pick(group_starts, owner)
    slot_index = owner * slot_count + within
    cell_ids = table_pick(star_cells.reshape(-1), slot_index)
    band_ids = table_pick(star_bands.reshape(-1), slot_index)
    cell_hot = cell_ids[:, None] == jnp.arange(cell_count, dtype=jnp.int32)[None, :]
    coef_rows = jnp.dot(
        cell_hot.astype(BF16), coef_table, preferred_element_type=F32
    ).astype(BF16)

    def mine(values):
        return lax.dynamic_slice_in_dim(values, my_group * lanes, lanes, 0)

    wavelength = 0.55 + 0.35 * band_ids.astype(F32) / (BANDS - 1)
    turns = phase_turns(mine(1.0 / wavelength), mine(coef_rows), feature_maps)
    turns = lax.all_to_all(turns, "row", split_axis=0, concat_axis=0, tiled=True)
    cotangent = jnp.take(
        incoming, mine(owner) * capacity + mine(within) // groups, axis=0, mode="clip"
    )
    cotangent = lax.all_to_all(cotangent, "row", split_axis=0, concat_axis=0, tiled=True)
    wave = wave_numbers(band_ids)
    my_wave = lax.dynamic_slice_in_dim(wave, my_group * lanes + my_lane, 1, 0)
    right, left = quarter_tables(size)
    path_grad = star_gradient(
        my_wave, turns.reshape(size, size), cotangent.reshape(size, size), right, left
    )
    path_grad = lax.all_to_all(
        path_grad.reshape(lanes, row_count, size), "row", split_axis=0, concat_axis=0, tiled=True
    )
    path_grads = lax.all_gather(path_grad, "star", axis=0, tiled=True)
    my_coefs = lax.dynamic_slice_in_dim(coef_rows.T, my_group * share, share, 0)
    map_grad, scores = map_sums(my_group, my_coefs, path_grads, feature_maps, share)
    coef_part = lax.dot_general(
        cell_hot.astype(F32),
        scores * (1.0 / (8 * size)),
        (((0,), (1,)), ((), ())),
        precision=lax.Precision.HIGHEST,
    )
    placed = lax.dynamic_update_slice_in_dim(
        jnp.zeros((cell_count, map_count), F32), coef_part, my_group * share, 1
    )
    return map_grad, lax.psum(placed, ("star", "row"))


def solution(mesh):
    placed = (P(None, "row", None), P(), P(), P(), P(), P("star", "row", None))
    device = star_devices if mesh.shape["row"] == LIVE_DEV else per_device
    return jax.shard_map(
        device,
        mesh=mesh,
        in_specs=placed,
        out_specs=(P("star", "row", None), P()),
        check_vma=False,
    )
```

```python
import functools

import jax
import jax.numpy as jnp
import numpy as np
from jax import lax
from jax.experimental import pallas as pl
from jax.experimental.pallas import tpu as pltpu
from jax.sharding import PartitionSpec as P

BANDS = 8
LIVE_DEV = 4
PLANE_DEV = 8
RADIX = 4
ROWS_STEP = 16
F32 = jnp.float32
BF16 = jnp.bfloat16


def fourier_tables(pupil_size):
    index_row = jnp.arange(pupil_size, dtype=jnp.int32)
    products = index_row[:, None] * index_row[None, :] % pupil_size
    angles = 2.0 * jnp.pi / pupil_size * products.astype(jnp.float32)
    return (jnp.cos(angles).astype(jnp.bfloat16), (-jnp.sin(angles)).astype(jnp.bfloat16))


def aperture_rows(first_row, row_count, pupil_size):
    centre = 0.5 * (pupil_size - 1)
    row_pos = (first_row + jnp.arange(row_count, dtype=jnp.int32)).astype(jnp.float32) - centre
    col_pos = jnp.arange(pupil_size, dtype=jnp.int32).astype(jnp.float32) - centre
    radius = row_pos[:, None] * row_pos[:, None] + col_pos[None, :] * col_pos[None, :]
    return jnp.where(radius <= 0.25 * pupil_size * pupil_size, 1.0, 0.0).astype(jnp.float32)


def wave_numbers(band_ids):
    wavelength = 0.55 + 0.35 * band_ids.astype(jnp.float32) / (BANDS - 1)
    return 2.0 * jnp.pi / wavelength


def table_pick(values, indices):
    positions = jnp.arange(values.shape[0], dtype=jnp.int32)
    chosen = jnp.where(positions[None, :] == indices[:, None], values[None, :], 0)
    return jnp.sum(chosen, axis=1)


def per_device(feature_maps, coef_table, star_counts, star_cells, star_bands, psf_cotangent):
    groups = lax.axis_size("star")
    my_group = lax.axis_index("star")
    slot_count = psf_cotangent.shape[0]
    map_count, row_count, pupil_size = feature_maps.shape
    group_ends = jnp.cumsum(star_counts)
    group_starts = group_ends - star_counts
    flat_cells = star_cells.reshape(-1)
    flat_bands = star_bands.reshape(-1)
    cell_count = coef_table.shape[0]
    capacity = -(-slot_count // groups)
    targets = jnp.arange(groups, dtype=jnp.int32)
    lane_index = jnp.arange(capacity, dtype=jnp.int32)
    my_start = table_pick(group_starts, my_group[None])
    my_count = table_pick(star_counts, my_group[None])
    first_slot = (targets - my_start) % groups
    send_slot = (first_slot[:, None] + lane_index[None, :] * groups).reshape(-1)
    valid_mask = send_slot < my_count
    picked = jnp.take(psf_cotangent, jnp.minimum(send_slot, slot_count - 1), axis=0)
    outgoing = jnp.where(valid_mask[:, None, None], picked, jnp.zeros_like(picked))
    incoming = lax.all_to_all(outgoing, "star", split_axis=0, concat_axis=0, tiled=True)
    star_rank = my_group + jnp.arange(LIVE_DEV, dtype=jnp.int32) * groups
    owner_group = jnp.sum((group_ends[None, :] <= star_rank[:, None]).astype(jnp.int32), axis=1)
    within = star_rank - table_pick(group_starts, owner_group)
    live_mask = jnp.ones((LIVE_DEV,), dtype=bool)
    owner_group, within, live_mask = (owner_group, within, live_mask)
    cotangent = jnp.take(incoming, owner_group * capacity + within // groups, axis=0)
    slot_index = owner_group * slot_count + within
    cell_ids = table_pick(flat_cells, slot_index)
    band_ids = table_pick(flat_bands, slot_index)
    cell_hot = cell_ids[:, None] == jnp.arange(cell_count, dtype=jnp.int32)[None, :]
    coef_rows = jnp.dot(
        cell_hot.astype(jnp.bfloat16), coef_table, preferred_element_type=jnp.float32
    ).astype(jnp.bfloat16)
    flat_maps = feature_maps.reshape(map_count, row_count * pupil_size)
    path_error = jnp.dot(coef_rows, flat_maps, preferred_element_type=jnp.float32).reshape(
        -1, row_count, pupil_size
    )
    wave_number = wave_numbers(band_ids)
    phase_angle = wave_number[:, None, None] * path_error
    aperture = aperture_rows(lax.axis_index("row") * row_count, row_count, pupil_size)
    cos_phase = jnp.cos(phase_angle)
    sin_phase = jnp.sin(phase_angle)
    pupil_field = jnp.stack([aperture * cos_phase, aperture * sin_phase], 1).astype(jnp.bfloat16)
    cos_table, sin_table = fourier_tables(pupil_size)
    inverse = 1.0 / pupil_size
    along_cos = jnp.einsum(
        "sarc,cv->sarv", pupil_field, cos_table, preferred_element_type=jnp.float32
    )
    along_sin = jnp.einsum(
        "sarc,cv->sarv", pupil_field, sin_table, preferred_element_type=jnp.float32
    )
    column_field = jnp.stack(
        [along_cos[:, 0] - along_sin[:, 1], along_sin[:, 0] + along_cos[:, 1]], 1
    ).astype(jnp.bfloat16)
    pieces = lax.all_to_all(column_field, "row", split_axis=3, concat_axis=2, tiled=True)
    row_cos = jnp.einsum("sarv,ru->savu", pieces, cos_table, preferred_element_type=jnp.float32)
    row_sin = jnp.einsum("sarv,ru->savu", pieces, sin_table, preferred_element_type=jnp.float32)
    real_part = (row_cos[:, 0] - row_sin[:, 1]) * inverse
    imag_part = (row_sin[:, 0] + row_cos[:, 1]) * inverse
    focal_field = jnp.stack([real_part, imag_part], 1)
    weight = jnp.where(live_mask, 2.0, 0.0).astype(jnp.float32)[:, None, None, None]
    focal_grad = (weight * cotangent.astype(jnp.float32)[:, None] * focal_field).astype(
        jnp.bfloat16
    )
    back_cos = jnp.einsum(
        "savu,ur->savr", focal_grad, cos_table, preferred_element_type=jnp.float32
    )
    back_sin = jnp.einsum(
        "savu,ur->savr", focal_grad, sin_table, preferred_element_type=jnp.float32
    )
    spectrum_grad = jnp.stack(
        [(back_cos[:, 0] + back_sin[:, 1]) * inverse, (back_cos[:, 1] - back_sin[:, 0]) * inverse],
        1,
    ).astype(jnp.bfloat16)
    pieces = lax.all_to_all(spectrum_grad, "row", split_axis=3, concat_axis=2, tiled=True)
    col_cos = jnp.einsum("savr,vc->sarc", pieces, cos_table, preferred_element_type=jnp.float32)
    col_sin = jnp.einsum("savr,vc->sarc", pieces, sin_table, preferred_element_type=jnp.float32)
    pupil_grad = jnp.stack([col_cos[:, 0] + col_sin[:, 1], col_cos[:, 1] - col_sin[:, 0]], 1)
    phase_grad = aperture * (cos_phase * pupil_grad[:, 1] - sin_phase * pupil_grad[:, 0])
    path_grad = (
        (wave_number[:, None, None] * phase_grad)
        .astype(jnp.bfloat16)
        .reshape(-1, row_count * pupil_size)
    )
    map_scores = lax.dot_general(
        path_grad, flat_maps, (((1,), (1,)), ((), ())), preferred_element_type=jnp.float32
    )
    coef_part = lax.dot_general(
        cell_hot.astype(jnp.float32),
        map_scores * (1.0 / (8 * pupil_size)),
        (((0,), (0,)), ((), ())),
        precision=lax.Precision.HIGHEST,
    )
    coef_grad = lax.psum(coef_part, ("star", "row"))
    share = map_count // groups
    map_grad = lax.psum_scatter(
        lax.dot_general(
            coef_rows, path_grad, (((0,), (0,)), ((), ())), preferred_element_type=jnp.float32
        ),
        "star",
        scatter_dimension=0,
        tiled=True,
    )
    return (map_grad.reshape(share, row_count, pupil_size), coef_grad)


def quarter_tables(size):
    quarter = size // RADIX
    place = np.arange(quarter)[None, :, None]
    freq = RADIX * np.arange(quarter)[None, None, :] + np.arange(RADIX)[:, None, None]
    angle = 2.0 * np.pi / size * ((place * freq) % size)
    cosine, sine = np.cos(angle), -np.sin(angle)
    right = np.concatenate(
        [np.concatenate([cosine, sine], 2), np.concatenate([-sine, cosine], 2)], 1
    ).astype(np.float32)
    left = np.swapaxes(right, 1, 2)
    return jnp.asarray(right.astype(jnp.bfloat16)), jnp.asarray(left.astype(jnp.bfloat16))


def turn_cos_sin(turns):
    half = turns * np.float32(np.pi)
    square = half * half
    sine = jnp.full_like(square, -1.0 / 39916800.0)
    for term in (1.0 / 362880.0, -1.0 / 5040.0, 1.0 / 120.0, -1.0 / 6.0, 1.0):
        sine = sine * square + np.float32(term)
    sine = sine * half
    cosine = jnp.full_like(square, 1.0 / 479001600.0)
    for term in (-1.0 / 3628800.0, 1.0 / 40320.0, -1.0 / 720.0, 1.0 / 24.0, -0.5, 1.0):
        cosine = cosine * square + np.float32(term)
    return 1.0 - 2.0 * sine * sine, 2.0 * sine * cosine


def butterfly(real, imag, sign):
    sr, dr = real[0] + real[2], real[0] - real[2]
    si, di = imag[0] + imag[2], imag[0] - imag[2]
    tr, er = real[1] + real[3], real[1] - real[3]
    ti, ei = imag[1] + imag[3], imag[1] - imag[3]
    if sign < 0:
        er, ei = -er, -ei
    return (
        [sr + tr, dr - ei, sr - tr, dr + ei],
        [si + ti, di + er, si - ti, di - er],
    )


def phase_kernel(inverse_ref, weight_ref, maps_ref, out_ref):
    stars, rows, size = out_ref.shape
    maps = maps_ref[...].reshape(maps_ref.shape[0] * rows, size)
    path = jnp.dot(weight_ref[...], maps, preferred_element_type=F32)
    for star in range(stars):
        turns = path[star * rows : (star + 1) * rows] * inverse_ref[star]
        out_ref[star] = (turns - jnp.floor(turns + 0.5)).astype(BF16)


def phase_turns(inverse_wave, coef_rows, feature_maps):
    map_count, row_count, size = feature_maps.shape
    stars = coef_rows.shape[0]
    weights = spread_rows(coef_rows)
    return pl.pallas_call(
        phase_kernel,
        out_shape=jax.ShapeDtypeStruct((stars, row_count, size), BF16),
        grid=(row_count // ROWS_STEP,),
        in_specs=[
            pl.BlockSpec(memory_space=pltpu.SMEM),
            pl.BlockSpec(weights.shape, lambda i: (0, 0)),
            pl.BlockSpec((map_count, ROWS_STEP, size), lambda i: (0, i, 0)),
        ],
        out_specs=pl.BlockSpec((stars, ROWS_STEP, size), lambda i: (0, i, 0)),
        cost_estimate=pl.CostEstimate(
            flops=2 * stars * ROWS_STEP * map_count * row_count * size,
            bytes_accessed=2 * (map_count + stars) * row_count * size,
            transcendentals=0,
        ),
        compiler_params=pltpu.CompilerParams(vmem_limit_bytes=24 << 20),
        name="phase_turns",
    )(inverse_wave, weights, feature_maps)


def spread_rows(weights):
    eye = jnp.eye(ROWS_STEP, dtype=weights.dtype)
    outs, ins = weights.shape
    spread = weights[:, None, :, None] * eye[None, :, None, :]
    return spread.reshape(outs * ROWS_STEP, ins * ROWS_STEP)


def star_kernel(
    chunk, wave_ref, turns_ref, cot_ref, right_ref, left_ref, out_ref, pr, pi, yr, yi, ct, xr, xi
):
    size = turns_ref.shape[1]
    quarter = size // RADIX
    steps = size // chunk
    blocks = [slice(m * quarter, (m + 1) * quarter) for m in range(RADIX)]
    centre = 0.5 * (size - 1)
    scale = 1.0 / size

    def forward_columns(step, carry):
        rows = pl.ds(pl.multiple_of(step * chunk, chunk), chunk)
        cosine, sine = turn_cos_sin(turns_ref[rows, :].astype(F32))
        row_pos = (
            lax.broadcasted_iota(jnp.int32, (chunk, size), 0) + step * chunk
        ).astype(F32) - centre
        col_pos = lax.broadcasted_iota(jnp.int32, (chunk, size), 1).astype(F32) - centre
        inside = row_pos * row_pos + col_pos * col_pos <= 0.25 * size * size
        real = jnp.where(inside, cosine, 0.0)
        imag = jnp.where(inside, sine, 0.0)
        pr[rows, :] = real
        pi[rows, :] = imag
        mixed_real, mixed_imag = butterfly(
            [real[:, b] for b in blocks], [imag[:, b] for b in blocks], -1
        )
        for k in range(RADIX):
            both = jnp.concatenate([mixed_real[k].astype(BF16), mixed_imag[k].astype(BF16)], 1)
            made = jnp.dot(both, right_ref[k], preferred_element_type=F32).astype(BF16)
            yr[rows, blocks[k]] = made[:, :quarter]
            yi[rows, blocks[k]] = made[:, quarter:]
        return carry

    lax.fori_loop(0, steps, forward_columns, 0)

    def pick(k):
        j = lax.broadcasted_iota(jnp.int32, (quarter, size), 0)
        f = lax.broadcasted_iota(jnp.int32, (quarter, size), 1)
        return jnp.where(f == RADIX * j + k, 1.0, 0.0).astype(BF16)

    nt = (((1,), (1,)), ((), ()))
    for k in range(RADIX):
        part = lax.dot_general(
            pick(k), cot_ref[...], nt, preferred_element_type=F32
        ).astype(BF16)
        for m in range(RADIX):
            ct[blocks[k], blocks[m]] = lax.dot_general(
                part, pick(m), nt, preferred_element_type=F32
            )

    def focal(step, carry):
        cols = pl.ds(pl.multiple_of(step * quarter, quarter), quarter)
        mixed_real, mixed_imag = butterfly(
            [yr[b, cols].astype(F32) for b in blocks],
            [yi[b, cols].astype(F32) for b in blocks],
            -1,
        )
        back_real, back_imag = [], []
        for k in range(RADIX):
            both = jnp.concatenate([mixed_real[k].astype(BF16), mixed_imag[k].astype(BF16)], 0)
            field = jnp.dot(left_ref[k], both, preferred_element_type=F32)
            weight = ct[blocks[k], cols] * (2.0 * scale)
            grad = (field * jnp.concatenate([weight, weight], 0)).astype(BF16)
            back = jnp.dot(right_ref[k], grad, preferred_element_type=F32)
            back_real.append(back[:quarter])
            back_imag.append(back[quarter:])
        spec_real, spec_imag = butterfly(back_real, back_imag, 1)
        for m in range(RADIX):
            xr[blocks[m], cols] = (spec_real[m] * scale).astype(BF16)
            xi[blocks[m], cols] = (spec_imag[m] * scale).astype(BF16)
        return carry

    lax.fori_loop(0, RADIX, focal, 0)

    def inverse_columns(step, carry):
        rows = pl.ds(pl.multiple_of(step * chunk, chunk), chunk)
        part_real, part_imag = [], []
        for k in range(RADIX):
            both = jnp.concatenate([xr[rows, blocks[k]], xi[rows, blocks[k]]], 1)
            made = jnp.dot(both, left_ref[k], preferred_element_type=F32)
            part_real.append(made[:, :quarter])
            part_imag.append(made[:, quarter:])
        grad_real, grad_imag = butterfly(part_real, part_imag, 1)
        wave = wave_ref[0]
        for m in range(RADIX):
            grad = pr[rows, blocks[m]] * grad_imag[m] - pi[rows, blocks[m]] * grad_real[m]
            out_ref[rows, blocks[m]] = (wave * grad).astype(BF16)
        return carry

    lax.fori_loop(0, steps, inverse_columns, 0)


def star_gradient(wave, turns, cotangent, right, left):
    size = turns.shape[0]
    vmem = pl.BlockSpec(memory_space=pltpu.VMEM)
    square = (size, size)
    return pl.pallas_call(
        functools.partial(star_kernel, 128),
        out_shape=jax.ShapeDtypeStruct(square, BF16),
        in_specs=[pl.BlockSpec(memory_space=pltpu.SMEM), vmem, vmem, vmem, vmem],
        out_specs=vmem,
        scratch_shapes=[
            pltpu.VMEM(square, F32),
            pltpu.VMEM(square, F32),
            pltpu.VMEM(square, BF16),
            pltpu.VMEM(square, BF16),
            pltpu.VMEM(square, F32),
            pltpu.VMEM(square, BF16),
            pltpu.VMEM(square, BF16),
        ],
        compiler_params=pltpu.CompilerParams(vmem_limit_bytes=56 << 20),
        name="star_gradient",
    )(wave, turns, cotangent, right, left)


def maps_kernel(group_ref, weight_ref, grad_ref, maps_ref, out_ref, score_ref):
    share, rows, size = out_ref.shape
    grads = grad_ref[...].reshape(grad_ref.shape[0] * rows, size)
    maps = maps_ref[...].reshape(share * rows, size)
    total = jnp.dot(weight_ref[...], grads, preferred_element_type=F32)
    out_ref[...] = total.reshape(share, rows, size)

    @pl.when(pl.program_id(0) == 0)
    def _():
        score_ref[...] = jnp.zeros_like(score_ref)

    score_ref[...] += lax.dot_general(
        maps, grads, (((1,), (1,)), ((), ())), preferred_element_type=F32
    )


def map_sums(my_group, coef_rows, path_grads, feature_maps, share):
    stars, row_count, size = path_grads.shape
    weights = spread_rows(coef_rows)
    score_shape = (share * ROWS_STEP, stars * ROWS_STEP)
    map_grad, scores = pl.pallas_call(
        maps_kernel,
        out_shape=(
            jax.ShapeDtypeStruct((share, row_count, size), F32),
            jax.ShapeDtypeStruct(score_shape, F32),
        ),
        grid_spec=pltpu.PrefetchScalarGridSpec(
            num_scalar_prefetch=1,
            grid=(row_count // ROWS_STEP,),
            in_specs=[
                pl.BlockSpec(weights.shape, lambda i, g: (0, 0)),
                pl.BlockSpec((stars, ROWS_STEP, size), lambda i, g: (0, i, 0)),
                pl.BlockSpec((share, ROWS_STEP, size), lambda i, g: (g[0], i, 0)),
            ],
            out_specs=(
                pl.BlockSpec((share, ROWS_STEP, size), lambda i, g: (0, i, 0)),
                pl.BlockSpec(score_shape, lambda i, g: (0, 0)),
            ),
        ),
        compiler_params=pltpu.CompilerParams(vmem_limit_bytes=24 << 20),
        name="map_sums",
    )(my_group[None], weights, path_grads, feature_maps)
    eye = jnp.eye(ROWS_STEP, dtype=F32)
    scores = scores.reshape(share, ROWS_STEP, stars, ROWS_STEP)
    return map_grad, jnp.sum(scores * eye[None, :, None, :], axis=(1, 3))


GATHER_STEPS = 8


def greet(peers):
    barrier = pltpu.get_barrier_semaphore()
    for peer in peers:
        pl.semaphore_signal(barrier, inc=1, device_id=peer, device_id_type=pl.DeviceIdType.MESH)
    pl.semaphore_wait(barrier, len(peers))


def send(source, target, send_sem, recv_sem, peer):
    return pltpu.make_async_remote_copy(
        src_ref=source,
        dst_ref=target,
        send_sem=send_sem,
        recv_sem=recv_sem,
        device_id=peer,
        device_id_type=pl.DeviceIdType.MESH,
    )


def row_kernel(lanes, in_ref, out_ref, local_sem, send_sem, recv_sem):
    row = lax.axis_index("row")
    peers = [{"row": (row + d) % lanes} for d in range(1, lanes)]
    greet(peers)
    copies = [
        send(
            in_ref.at[(row + d) % lanes],
            out_ref.at[row],
            send_sem.at[d - 1],
            recv_sem.at[d - 1],
            peers[d - 1],
        )
        for d in range(1, lanes)
    ]
    for copy in copies:
        copy.start()
    own = pltpu.make_async_copy(in_ref.at[row], out_ref.at[row], local_sem)
    own.start()
    own.wait()
    for copy in copies:
        copy.wait()


def row_exchange(blocks, collective_id):
    lanes = blocks.shape[0]
    return pl.pallas_call(
        functools.partial(row_kernel, lanes),
        out_shape=jax.ShapeDtypeStruct(blocks.shape, blocks.dtype),
        in_specs=[pl.BlockSpec(memory_space=pltpu.VMEM)],
        out_specs=pl.BlockSpec(memory_space=pl.ANY),
        scratch_shapes=[
            pltpu.SemaphoreType.DMA,
            pltpu.SemaphoreType.DMA((lanes - 1,)),
            pltpu.SemaphoreType.DMA((lanes - 1,)),
        ],
        compiler_params=pltpu.CompilerParams(
            collective_id=collective_id, has_side_effects=True, vmem_limit_bytes=8 << 20
        ),
        cost_estimate=pl.CostEstimate(
            flops=0, bytes_accessed=50 * blocks.size * 2, transcendentals=0
        ),
        name="row_exchange",
    )(blocks)


def gather_kernel(lanes, in_ref, out_ref, local, z_send, z_recv, p_send, p_recv, c_send, c_recv):
    row = lax.axis_index("row")
    me = lax.axis_index("star")
    depth = in_ref.shape[1] // GATHER_STEPS
    core = me + 1 - 2 * (me % 2)
    across = me + 2 - 4 * ((me // 2) % 2)
    along = me + 4 - 8 * ((me // 4) % 2)
    corner = across + 4 - 8 * ((me // 4) % 2)
    peers = [{"row": (row + d) % lanes} for d in range(1, lanes)]
    to_core, to_across, to_along = {"star": core}, {"star": across}, {"star": along}
    greet(peers + [to_core, to_across, to_along])
    half = lanes // 2
    started = []

    def start(copy):
        copy.start()
        started.append(copy)
        return copy

    def block(group, step, first=0, count=lanes):
        return out_ref.at[group, pl.ds(first, count), pl.ds(step * depth, depth)]

    own, exchanged = [], []
    for step in range(GATHER_STEPS):
        rows = pl.ds(step * depth, depth)
        copy = pltpu.make_async_copy(
            in_ref.at[row, rows], out_ref.at[me, row, rows], local.at[step]
        )
        copy.start()
        own.append(copy)
        exchanged.append(
            [
                start(
                    send(
                        in_ref.at[(row + d) % lanes, rows],
                        out_ref.at[me, row, rows],
                        z_send.at[step, d - 1],
                        z_recv.at[step, d - 1],
                        peers[d - 1],
                    )
                )
                for d in range(1, lanes)
            ]
        )

    def plane(step, way, part, peer):
        return start(send(part, part, p_send.at[step, way], p_recv.at[step, way], peer))

    def cores(step, way, part):
        return start(send(part, part, c_send.at[step, way], c_recv.at[step, way], to_core))

    sides, corners, twins = {}, {}, []
    for step in range(GATHER_STEPS + 2):
        if step < GATHER_STEPS:
            own[step].wait()
            for copy in exchanged[step]:
                copy.wait_recv()
            part = block(me, step)
            sides[step] = (
                plane(step, 0, part, to_across),
                plane(step, 1, part, to_along),
            )
            twins.append(cores(step, 0, part))
        last = step - 1
        if 0 <= last < GATHER_STEPS:
            sides[last][0].wait_recv()
            first = plane(last, 2, block(across, last, 0, half), to_along)
            twins.append(cores(last, 1, block(across, last)))
            sides[last][1].wait_recv()
            second = plane(last, 3, block(along, last, half, lanes - half), to_across)
            twins.append(cores(last, 2, block(along, last)))
            corners[last] = (first, second)
        last = step - 2
        if last >= 0:
            corners[last][0].wait_recv()
            corners[last][1].wait_recv()
            twins.append(cores(last, 3, block(corner, last)))
    for copy in twins:
        copy.wait_recv()
    for copy in started:
        copy.wait_send()


def gather_grads(path_grad, groups):
    lanes, row_count, size = path_grad.shape
    dma = pltpu.SemaphoreType.DMA
    return pl.pallas_call(
        functools.partial(gather_kernel, lanes),
        out_shape=jax.ShapeDtypeStruct((groups, lanes, row_count, size), path_grad.dtype),
        in_specs=[pl.BlockSpec(memory_space=pltpu.VMEM)],
        out_specs=pl.BlockSpec(memory_space=pl.ANY),
        scratch_shapes=[
            dma((GATHER_STEPS,)),
            dma((GATHER_STEPS, lanes - 1)),
            dma((GATHER_STEPS, lanes - 1)),
            dma((GATHER_STEPS, 4)),
            dma((GATHER_STEPS, 4)),
            dma((GATHER_STEPS, 4)),
            dma((GATHER_STEPS, 4)),
        ],
        compiler_params=pltpu.CompilerParams(
            collective_id=1, has_side_effects=True, vmem_limit_bytes=8 << 20
        ),
        name="gather_grads",
    )(path_grad)


def score_kernel(groups, lanes, in_ref, out_ref, z_send, z_recv, s_send, s_recv):
    row = lax.axis_index("row")
    me = lax.axis_index("star")
    row_peers = [{"row": (row + d) % lanes} for d in range(1, lanes)]
    star_peers = [{"star": (me + d) % groups} for d in range(1, groups)]
    greet(row_peers + star_peers)
    copies = [
        send(in_ref, out_ref.at[me, row], z_send.at[d], z_recv.at[d], row_peers[d])
        for d in range(lanes - 1)
    ]
    for copy in copies:
        copy.start()
    out_ref[me, row] = in_ref[...]
    for copy in copies:
        copy.wait()
    copies = [
        send(out_ref.at[me], out_ref.at[me], s_send.at[d], s_recv.at[d], star_peers[d])
        for d in range(groups - 1)
    ]
    for copy in copies:
        copy.start()
    for copy in copies:
        copy.wait()


def gather_scores(scores, groups, lanes):
    dma = pltpu.SemaphoreType.DMA
    vmem = pl.BlockSpec(memory_space=pltpu.VMEM)
    return pl.pallas_call(
        functools.partial(score_kernel, groups, lanes),
        out_shape=jax.ShapeDtypeStruct((groups, lanes) + scores.shape, scores.dtype),
        in_specs=[vmem],
        out_specs=vmem,
        scratch_shapes=[
            dma((lanes - 1,)),
            dma((lanes - 1,)),
            dma((groups - 1,)),
            dma((groups - 1,)),
        ],
        compiler_params=pltpu.CompilerParams(
            collective_id=2, has_side_effects=True, vmem_limit_bytes=8 << 20
        ),
        name="gather_scores",
    )(scores)


def star_devices(feature_maps, coef_table, star_counts, star_cells, star_bands, psf_cotangent):
    groups = lax.axis_size("star")
    lanes = lax.axis_size("row")
    my_group = lax.axis_index("star")
    my_lane = lax.axis_index("row")
    slot_count = psf_cotangent.shape[0]
    map_count, row_count, size = feature_maps.shape
    cell_count = coef_table.shape[0]
    share = map_count // groups
    group_ends = jnp.cumsum(star_counts)
    group_starts = group_ends - star_counts
    capacity = -(-slot_count // groups)
    targets = jnp.arange(groups, dtype=jnp.int32)
    my_start = table_pick(group_starts, my_group[None])
    first_slot = (targets - my_start) % groups
    lane_index = jnp.arange(capacity, dtype=jnp.int32)
    send_slot = (first_slot[:, None] + lane_index[None, :] * groups).reshape(-1)
    outgoing = jnp.take(
        psf_cotangent, jnp.minimum(send_slot, slot_count - 1), axis=0, mode="clip"
    )
    incoming = lax.all_to_all(outgoing, "star", split_axis=0, concat_axis=0, tiled=True)

    total = groups * lanes
    order = jnp.arange(total, dtype=jnp.int32)
    rank = order // lanes + (order % lanes) * groups
    owner = jnp.sum((group_ends[None, :] <= rank[:, None]).astype(jnp.int32), axis=1)
    within = rank - table_pick(group_starts, owner)
    slot_index = owner * slot_count + within
    cell_ids = table_pick(star_cells.reshape(-1), slot_index)
    band_ids = table_pick(star_bands.reshape(-1), slot_index)
    cell_hot = cell_ids[:, None] == jnp.arange(cell_count, dtype=jnp.int32)[None, :]
    coef_rows = jnp.dot(
        cell_hot.astype(BF16), coef_table, preferred_element_type=F32
    ).astype(BF16)

    def mine(values):
        return lax.dynamic_slice_in_dim(values, my_group * lanes, lanes, 0)

    wavelength = 0.55 + 0.35 * band_ids.astype(F32) / (BANDS - 1)
    turns = phase_turns(mine(1.0 / wavelength), mine(coef_rows), feature_maps)
    turns = row_exchange(turns, 0)
    incoming, turns = lax.optimization_barrier((incoming, turns))
    cotangent = jnp.take(
        incoming, mine(owner) * capacity + mine(within) // groups, axis=0, mode="clip"
    )
    cotangent = lax.all_to_all(cotangent, "row", split_axis=0, concat_axis=0, tiled=True)
    wave = wave_numbers(band_ids)
    my_wave = lax.dynamic_slice_in_dim(wave, my_group * lanes + my_lane, 1, 0)
    right, left = quarter_tables(size)
    path_grad = star_gradient(
        my_wave, turns.reshape(size, size), cotangent.reshape(size, size), right, left
    )
    path_grads = gather_grads(path_grad.reshape(lanes, row_count, size), groups)
    path_grads = path_grads.reshape(total, row_count, size)
    my_coefs = lax.dynamic_slice_in_dim(coef_rows.T, my_group * share, share, 0)
    map_grad, scores = map_sums(my_group, my_coefs, path_grads, feature_maps, share)
    scores = jnp.pad(scores, ((0, 0), (0, -total % 128)))
    scores = jnp.sum(gather_scores(scores, groups, lanes), axis=1)
    scores = scores.reshape(map_count, -1)[:, :total]
    coef_grad = lax.dot_general(
        cell_hot.astype(F32),
        scores * (1.0 / (8 * size)),
        (((0,), (1,)), ((), ())),
        precision=lax.Precision.HIGHEST,
    )
    return map_grad, coef_grad


def solution(mesh):
    placed = (P(None, "row", None), P(), P(), P(), P(), P("star", "row", None))
    fits = mesh.shape["row"] == LIVE_DEV and mesh.shape["star"] == PLANE_DEV
    device = star_devices if fits else per_device
    return jax.shard_map(
        device,
        mesh=mesh,
        in_specs=placed,
        out_specs=(P("star", "row", None), P()),
        check_vma=False,
    )
```

```python
import functools

import jax
import jax.numpy as jnp
import numpy as np
from jax import lax
from jax.experimental import pallas as pl
from jax.experimental.pallas import tpu as pltpu
from jax.sharding import PartitionSpec as P

BANDS = 8
LIVE_DEV = 4
PLANE_DEV = 8
RADIX = 4
ROWS_STEP = 16
F32 = jnp.float32
BF16 = jnp.bfloat16


def fourier_tables(pupil_size):
    index_row = jnp.arange(pupil_size, dtype=jnp.int32)
    products = index_row[:, None] * index_row[None, :] % pupil_size
    angles = 2.0 * jnp.pi / pupil_size * products.astype(jnp.float32)
    return (jnp.cos(angles).astype(jnp.bfloat16), (-jnp.sin(angles)).astype(jnp.bfloat16))


def aperture_rows(first_row, row_count, pupil_size):
    centre = 0.5 * (pupil_size - 1)
    row_pos = (first_row + jnp.arange(row_count, dtype=jnp.int32)).astype(jnp.float32) - centre
    col_pos = jnp.arange(pupil_size, dtype=jnp.int32).astype(jnp.float32) - centre
    radius = row_pos[:, None] * row_pos[:, None] + col_pos[None, :] * col_pos[None, :]
    return jnp.where(radius <= 0.25 * pupil_size * pupil_size, 1.0, 0.0).astype(jnp.float32)


def wave_numbers(band_ids):
    wavelength = 0.55 + 0.35 * band_ids.astype(jnp.float32) / (BANDS - 1)
    return 2.0 * jnp.pi / wavelength


def table_pick(values, indices):
    positions = jnp.arange(values.shape[0], dtype=jnp.int32)
    chosen = jnp.where(positions[None, :] == indices[:, None], values[None, :], 0)
    return jnp.sum(chosen, axis=1)


def per_device(feature_maps, coef_table, star_counts, star_cells, star_bands, psf_cotangent):
    groups = lax.axis_size("star")
    my_group = lax.axis_index("star")
    slot_count = psf_cotangent.shape[0]
    map_count, row_count, pupil_size = feature_maps.shape
    group_ends = jnp.cumsum(star_counts)
    group_starts = group_ends - star_counts
    flat_cells = star_cells.reshape(-1)
    flat_bands = star_bands.reshape(-1)
    cell_count = coef_table.shape[0]
    capacity = -(-slot_count // groups)
    targets = jnp.arange(groups, dtype=jnp.int32)
    lane_index = jnp.arange(capacity, dtype=jnp.int32)
    my_start = table_pick(group_starts, my_group[None])
    my_count = table_pick(star_counts, my_group[None])
    first_slot = (targets - my_start) % groups
    send_slot = (first_slot[:, None] + lane_index[None, :] * groups).reshape(-1)
    valid_mask = send_slot < my_count
    picked = jnp.take(psf_cotangent, jnp.minimum(send_slot, slot_count - 1), axis=0)
    outgoing = jnp.where(valid_mask[:, None, None], picked, jnp.zeros_like(picked))
    incoming = lax.all_to_all(outgoing, "star", split_axis=0, concat_axis=0, tiled=True)
    star_rank = my_group + jnp.arange(LIVE_DEV, dtype=jnp.int32) * groups
    owner_group = jnp.sum((group_ends[None, :] <= star_rank[:, None]).astype(jnp.int32), axis=1)
    within = star_rank - table_pick(group_starts, owner_group)
    live_mask = jnp.ones((LIVE_DEV,), dtype=bool)
    owner_group, within, live_mask = (owner_group, within, live_mask)
    cotangent = jnp.take(incoming, owner_group * capacity + within // groups, axis=0)
    slot_index = owner_group * slot_count + within
    cell_ids = table_pick(flat_cells, slot_index)
    band_ids = table_pick(flat_bands, slot_index)
    cell_hot = cell_ids[:, None] == jnp.arange(cell_count, dtype=jnp.int32)[None, :]
    coef_rows = jnp.dot(
        cell_hot.astype(jnp.bfloat16), coef_table, preferred_element_type=jnp.float32
    ).astype(jnp.bfloat16)
    flat_maps = feature_maps.reshape(map_count, row_count * pupil_size)
    path_error = jnp.dot(coef_rows, flat_maps, preferred_element_type=jnp.float32).reshape(
        -1, row_count, pupil_size
    )
    wave_number = wave_numbers(band_ids)
    phase_angle = wave_number[:, None, None] * path_error
    aperture = aperture_rows(lax.axis_index("row") * row_count, row_count, pupil_size)
    cos_phase = jnp.cos(phase_angle)
    sin_phase = jnp.sin(phase_angle)
    pupil_field = jnp.stack([aperture * cos_phase, aperture * sin_phase], 1).astype(jnp.bfloat16)
    cos_table, sin_table = fourier_tables(pupil_size)
    inverse = 1.0 / pupil_size
    along_cos = jnp.einsum(
        "sarc,cv->sarv", pupil_field, cos_table, preferred_element_type=jnp.float32
    )
    along_sin = jnp.einsum(
        "sarc,cv->sarv", pupil_field, sin_table, preferred_element_type=jnp.float32
    )
    column_field = jnp.stack(
        [along_cos[:, 0] - along_sin[:, 1], along_sin[:, 0] + along_cos[:, 1]], 1
    ).astype(jnp.bfloat16)
    pieces = lax.all_to_all(column_field, "row", split_axis=3, concat_axis=2, tiled=True)
    row_cos = jnp.einsum("sarv,ru->savu", pieces, cos_table, preferred_element_type=jnp.float32)
    row_sin = jnp.einsum("sarv,ru->savu", pieces, sin_table, preferred_element_type=jnp.float32)
    real_part = (row_cos[:, 0] - row_sin[:, 1]) * inverse
    imag_part = (row_sin[:, 0] + row_cos[:, 1]) * inverse
    focal_field = jnp.stack([real_part, imag_part], 1)
    weight = jnp.where(live_mask, 2.0, 0.0).astype(jnp.float32)[:, None, None, None]
    focal_grad = (weight * cotangent.astype(jnp.float32)[:, None] * focal_field).astype(
        jnp.bfloat16
    )
    back_cos = jnp.einsum(
        "savu,ur->savr", focal_grad, cos_table, preferred_element_type=jnp.float32
    )
    back_sin = jnp.einsum(
        "savu,ur->savr", focal_grad, sin_table, preferred_element_type=jnp.float32
    )
    spectrum_grad = jnp.stack(
        [(back_cos[:, 0] + back_sin[:, 1]) * inverse, (back_cos[:, 1] - back_sin[:, 0]) * inverse],
        1,
    ).astype(jnp.bfloat16)
    pieces = lax.all_to_all(spectrum_grad, "row", split_axis=3, concat_axis=2, tiled=True)
    col_cos = jnp.einsum("savr,vc->sarc", pieces, cos_table, preferred_element_type=jnp.float32)
    col_sin = jnp.einsum("savr,vc->sarc", pieces, sin_table, preferred_element_type=jnp.float32)
    pupil_grad = jnp.stack([col_cos[:, 0] + col_sin[:, 1], col_cos[:, 1] - col_sin[:, 0]], 1)
    phase_grad = aperture * (cos_phase * pupil_grad[:, 1] - sin_phase * pupil_grad[:, 0])
    path_grad = (
        (wave_number[:, None, None] * phase_grad)
        .astype(jnp.bfloat16)
        .reshape(-1, row_count * pupil_size)
    )
    map_scores = lax.dot_general(
        path_grad, flat_maps, (((1,), (1,)), ((), ())), preferred_element_type=jnp.float32
    )
    coef_part = lax.dot_general(
        cell_hot.astype(jnp.float32),
        map_scores * (1.0 / (8 * pupil_size)),
        (((0,), (0,)), ((), ())),
        precision=lax.Precision.HIGHEST,
    )
    coef_grad = lax.psum(coef_part, ("star", "row"))
    share = map_count // groups
    map_grad = lax.psum_scatter(
        lax.dot_general(
            coef_rows, path_grad, (((0,), (0,)), ((), ())), preferred_element_type=jnp.float32
        ),
        "star",
        scatter_dimension=0,
        tiled=True,
    )
    return (map_grad.reshape(share, row_count, pupil_size), coef_grad)


def quarter_tables(size):
    quarter = size // RADIX
    place = np.arange(quarter)[None, :, None]
    freq = RADIX * np.arange(quarter)[None, None, :] + np.arange(RADIX)[:, None, None]
    angle = 2.0 * np.pi / size * ((place * freq) % size)
    cosine, sine = np.cos(angle), -np.sin(angle)
    right = np.concatenate(
        [np.concatenate([cosine, sine], 2), np.concatenate([-sine, cosine], 2)], 1
    ).astype(np.float32)
    left = np.swapaxes(right, 1, 2)
    return jnp.asarray(right.astype(jnp.bfloat16)), jnp.asarray(left.astype(jnp.bfloat16))


def turn_cos_sin(turns):
    half = turns * np.float32(np.pi)
    square = half * half
    sine = jnp.full_like(square, -1.0 / 39916800.0)
    for term in (1.0 / 362880.0, -1.0 / 5040.0, 1.0 / 120.0, -1.0 / 6.0, 1.0):
        sine = sine * square + np.float32(term)
    sine = sine * half
    cosine = jnp.full_like(square, 1.0 / 479001600.0)
    for term in (-1.0 / 3628800.0, 1.0 / 40320.0, -1.0 / 720.0, 1.0 / 24.0, -0.5, 1.0):
        cosine = cosine * square + np.float32(term)
    return 1.0 - 2.0 * sine * sine, 2.0 * sine * cosine


def butterfly(real, imag, sign):
    sr, dr = real[0] + real[2], real[0] - real[2]
    si, di = imag[0] + imag[2], imag[0] - imag[2]
    tr, er = real[1] + real[3], real[1] - real[3]
    ti, ei = imag[1] + imag[3], imag[1] - imag[3]
    if sign < 0:
        er, ei = -er, -ei
    return (
        [sr + tr, dr - ei, sr - tr, dr + ei],
        [si + ti, di + er, si - ti, di - er],
    )


def phase_kernel(inverse_ref, weight_ref, maps_ref, out_ref):
    stars, rows, size = out_ref.shape
    maps = maps_ref[...].reshape(maps_ref.shape[0] * rows, size)
    path = jnp.dot(weight_ref[...], maps, preferred_element_type=F32)
    for star in range(stars):
        turns = path[star * rows : (star + 1) * rows] * inverse_ref[star]
        out_ref[star] = (turns - jnp.floor(turns + 0.5)).astype(BF16)


def phase_turns(inverse_wave, coef_rows, feature_maps):
    map_count, row_count, size = feature_maps.shape
    stars = coef_rows.shape[0]
    weights = spread_rows(coef_rows)
    return pl.pallas_call(
        phase_kernel,
        out_shape=jax.ShapeDtypeStruct((stars, row_count, size), BF16),
        grid=(row_count // ROWS_STEP,),
        in_specs=[
            pl.BlockSpec(memory_space=pltpu.SMEM),
            pl.BlockSpec(weights.shape, lambda i: (0, 0)),
            pl.BlockSpec((map_count, ROWS_STEP, size), lambda i: (0, i, 0)),
        ],
        out_specs=pl.BlockSpec((stars, ROWS_STEP, size), lambda i: (0, i, 0)),
        cost_estimate=pl.CostEstimate(
            flops=2 * stars * ROWS_STEP * map_count * row_count * size,
            bytes_accessed=2 * (map_count + stars) * row_count * size,
            transcendentals=0,
        ),
        compiler_params=pltpu.CompilerParams(vmem_limit_bytes=24 << 20),
        name="phase_turns",
    )(inverse_wave, weights, feature_maps)


def spread_rows(weights):
    eye = jnp.eye(ROWS_STEP, dtype=weights.dtype)
    outs, ins = weights.shape
    spread = weights[:, None, :, None] * eye[None, :, None, :]
    return spread.reshape(outs * ROWS_STEP, ins * ROWS_STEP)


def star_kernel(
    chunk, wave_ref, turns_ref, cot_ref, right_ref, left_ref, out_ref, pr, pi, yr, yi, ct, xr, xi
):
    size = turns_ref.shape[1]
    quarter = size // RADIX
    steps = size // chunk
    blocks = [slice(m * quarter, (m + 1) * quarter) for m in range(RADIX)]
    centre = 0.5 * (size - 1)
    scale = 1.0 / size

    def forward_columns(step, carry):
        rows = pl.ds(pl.multiple_of(step * chunk, chunk), chunk)
        cosine, sine = turn_cos_sin(turns_ref[rows, :].astype(F32))
        row_pos = (
            lax.broadcasted_iota(jnp.int32, (chunk, size), 0) + step * chunk
        ).astype(F32) - centre
        col_pos = lax.broadcasted_iota(jnp.int32, (chunk, size), 1).astype(F32) - centre
        inside = row_pos * row_pos + col_pos * col_pos <= 0.25 * size * size
        real = jnp.where(inside, cosine, 0.0)
        imag = jnp.where(inside, sine, 0.0)
        pr[rows, :] = real
        pi[rows, :] = imag
        mixed_real, mixed_imag = butterfly(
            [real[:, b] for b in blocks], [imag[:, b] for b in blocks], -1
        )
        for k in range(RADIX):
            both = jnp.concatenate([mixed_real[k].astype(BF16), mixed_imag[k].astype(BF16)], 1)
            made = jnp.dot(both, right_ref[k], preferred_element_type=F32).astype(BF16)
            yr[rows, blocks[k]] = made[:, :quarter]
            yi[rows, blocks[k]] = made[:, quarter:]
        return carry

    lax.fori_loop(0, steps, forward_columns, 0)

    def pick(k):
        j = lax.broadcasted_iota(jnp.int32, (quarter, size), 0)
        f = lax.broadcasted_iota(jnp.int32, (quarter, size), 1)
        return jnp.where(f == RADIX * j + k, 1.0, 0.0).astype(BF16)

    nt = (((1,), (1,)), ((), ()))
    for k in range(RADIX):
        part = lax.dot_general(
            pick(k), cot_ref[...], nt, preferred_element_type=F32
        ).astype(BF16)
        for m in range(RADIX):
            ct[blocks[k], blocks[m]] = lax.dot_general(
                part, pick(m), nt, preferred_element_type=F32
            )

    def focal(step, carry):
        cols = pl.ds(pl.multiple_of(step * quarter, quarter), quarter)
        mixed_real, mixed_imag = butterfly(
            [yr[b, cols].astype(F32) for b in blocks],
            [yi[b, cols].astype(F32) for b in blocks],
            -1,
        )
        back_real, back_imag = [], []
        for k in range(RADIX):
            both = jnp.concatenate([mixed_real[k].astype(BF16), mixed_imag[k].astype(BF16)], 0)
            field = jnp.dot(left_ref[k], both, preferred_element_type=F32)
            weight = ct[blocks[k], cols] * (2.0 * scale)
            grad = (field * jnp.concatenate([weight, weight], 0)).astype(BF16)
            back = jnp.dot(right_ref[k], grad, preferred_element_type=F32)
            back_real.append(back[:quarter])
            back_imag.append(back[quarter:])
        spec_real, spec_imag = butterfly(back_real, back_imag, 1)
        for m in range(RADIX):
            xr[blocks[m], cols] = (spec_real[m] * scale).astype(BF16)
            xi[blocks[m], cols] = (spec_imag[m] * scale).astype(BF16)
        return carry

    lax.fori_loop(0, RADIX, focal, 0)

    def inverse_columns(step, carry):
        rows = pl.ds(pl.multiple_of(step * chunk, chunk), chunk)
        part_real, part_imag = [], []
        for k in range(RADIX):
            both = jnp.concatenate([xr[rows, blocks[k]], xi[rows, blocks[k]]], 1)
            made = jnp.dot(both, left_ref[k], preferred_element_type=F32)
            part_real.append(made[:, :quarter])
            part_imag.append(made[:, quarter:])
        grad_real, grad_imag = butterfly(part_real, part_imag, 1)
        wave = wave_ref[0]
        for m in range(RADIX):
            grad = pr[rows, blocks[m]] * grad_imag[m] - pi[rows, blocks[m]] * grad_real[m]
            out_ref[rows, blocks[m]] = (wave * grad).astype(BF16)
        return carry

    lax.fori_loop(0, steps, inverse_columns, 0)


def star_gradient(wave, turns, cotangent, right, left):
    size = turns.shape[0]
    vmem = pl.BlockSpec(memory_space=pltpu.VMEM)
    square = (size, size)
    return pl.pallas_call(
        functools.partial(star_kernel, 128),
        out_shape=jax.ShapeDtypeStruct(square, BF16),
        in_specs=[pl.BlockSpec(memory_space=pltpu.SMEM), vmem, vmem, vmem, vmem],
        out_specs=vmem,
        scratch_shapes=[
            pltpu.VMEM(square, F32),
            pltpu.VMEM(square, F32),
            pltpu.VMEM(square, BF16),
            pltpu.VMEM(square, BF16),
            pltpu.VMEM(square, F32),
            pltpu.VMEM(square, BF16),
            pltpu.VMEM(square, BF16),
        ],
        compiler_params=pltpu.CompilerParams(vmem_limit_bytes=56 << 20),
        name="star_gradient",
    )(wave, turns, cotangent, right, left)


def maps_kernel(group_ref, weight_ref, grad_ref, maps_ref, out_ref, score_ref):
    share, rows, size = out_ref.shape
    grads = grad_ref[...].reshape(grad_ref.shape[0] * rows, size)
    maps = maps_ref[...].reshape(share * rows, size)
    total = jnp.dot(weight_ref[...], grads, preferred_element_type=F32)
    out_ref[...] = total.reshape(share, rows, size)

    @pl.when(pl.program_id(0) == 0)
    def _():
        score_ref[...] = jnp.zeros_like(score_ref)

    score_ref[...] += lax.dot_general(
        maps, grads, (((1,), (1,)), ((), ())), preferred_element_type=F32
    )


def map_sums(my_group, coef_rows, path_grads, feature_maps, share):
    stars, row_count, size = path_grads.shape
    weights = spread_rows(coef_rows)
    score_shape = (share * ROWS_STEP, stars * ROWS_STEP)
    map_grad, scores = pl.pallas_call(
        maps_kernel,
        out_shape=(
            jax.ShapeDtypeStruct((share, row_count, size), F32),
            jax.ShapeDtypeStruct(score_shape, F32),
        ),
        grid_spec=pltpu.PrefetchScalarGridSpec(
            num_scalar_prefetch=1,
            grid=(row_count // ROWS_STEP,),
            in_specs=[
                pl.BlockSpec(weights.shape, lambda i, g: (0, 0)),
                pl.BlockSpec((stars, ROWS_STEP, size), lambda i, g: (0, i, 0)),
                pl.BlockSpec((share, ROWS_STEP, size), lambda i, g: (g[0], i, 0)),
            ],
            out_specs=(
                pl.BlockSpec((share, ROWS_STEP, size), lambda i, g: (0, i, 0)),
                pl.BlockSpec(score_shape, lambda i, g: (0, 0)),
            ),
        ),
        compiler_params=pltpu.CompilerParams(vmem_limit_bytes=24 << 20),
        name="map_sums",
    )(my_group[None], weights, path_grads, feature_maps)
    eye = jnp.eye(ROWS_STEP, dtype=F32)
    scores = scores.reshape(share, ROWS_STEP, stars, ROWS_STEP)
    return map_grad, jnp.sum(scores * eye[None, :, None, :], axis=(1, 3))


GATHER_STEPS = 8


def greet(peers):
    barrier = pltpu.get_barrier_semaphore()
    for peer in peers:
        pl.semaphore_signal(barrier, inc=1, device_id=peer, device_id_type=pl.DeviceIdType.MESH)
    pl.semaphore_wait(barrier, len(peers))


def send(source, target, send_sem, recv_sem, peer):
    return pltpu.make_async_remote_copy(
        src_ref=source,
        dst_ref=target,
        send_sem=send_sem,
        recv_sem=recv_sem,
        device_id=peer,
        device_id_type=pl.DeviceIdType.MESH,
    )


DELIVER_STEPS = 4


def deliver_kernel(
    groups, lanes, pick_ref, turns_ref, cot_ref, turns_out, cot_out, stage, *scratch
):
    arrived, sems = scratch[:DELIVER_STEPS], scratch[DELIVER_STEPS:]
    t_local, t_send, t_recv, s_local, s_send, s_recv, z_local, z_send, z_recv = sems
    row = lax.axis_index("row")
    me = lax.axis_index("star")
    capacity = cot_ref.shape[1]
    depth = cot_ref.shape[2] // DELIVER_STEPS
    row_peers = [{"row": (row + d) % lanes} for d in range(1, lanes)]
    star_peers = [{"star": (me + d) % groups} for d in range(1, groups)]
    greet(row_peers + star_peers)
    turns = [
        send(
            turns_ref.at[(row + d) % lanes],
            turns_out.at[row],
            t_send.at[d - 1],
            t_recv.at[d - 1],
            row_peers[d - 1],
        )
        for d in range(1, lanes)
    ]
    turns.append(pltpu.make_async_copy(turns_ref.at[row], turns_out.at[row], t_local))
    for copy in turns:
        copy.start()
    steps = []
    for step in range(DELIVER_STEPS):
        rows = pl.ds(step * depth, depth)
        target = arrived[step].at[pl.ds(me * capacity, capacity)]
        copies = [
            send(
                cot_ref.at[(me + d) % groups, :, rows],
                target,
                s_send.at[step, d - 1],
                s_recv.at[step, d - 1],
                star_peers[d - 1],
            )
            for d in range(1, groups)
        ]
        copies.append(pltpu.make_async_copy(cot_ref.at[me, :, rows], target, s_local.at[step]))
        for copy in copies:
            copy.start()
        steps.append(copies)
    sent = []
    for step in range(DELIVER_STEPS):
        rows = pl.ds(step * depth, depth)
        for copy in steps[step]:
            copy.wait()
        for lane in range(lanes):
            stage[lane, rows] = arrived[step][pick_ref[lane]]
        copies = [
            send(
                stage.at[(row + d) % lanes, rows],
                cot_out.at[row, rows],
                z_send.at[step, d - 1],
                z_recv.at[step, d - 1],
                row_peers[d - 1],
            )
            for d in range(1, lanes)
        ]
        copies.append(
            pltpu.make_async_copy(stage.at[row, rows], cot_out.at[row, rows], z_local.at[step])
        )
        for copy in copies:
            copy.start()
        sent += copies
    for copy in turns + sent:
        copy.wait()


def deliver(picks, turns, outgoing):
    groups, capacity, row_count, size = outgoing.shape
    lanes = turns.shape[0]
    depth = row_count // DELIVER_STEPS
    dma = pltpu.SemaphoreType.DMA
    hbm = pl.BlockSpec(memory_space=pl.ANY)
    vmem = pl.BlockSpec(memory_space=pltpu.VMEM)
    shape = jax.ShapeDtypeStruct((lanes, row_count, size), BF16)
    return pl.pallas_call(
        functools.partial(deliver_kernel, groups, lanes),
        out_shape=(shape, shape),
        in_specs=[pl.BlockSpec(memory_space=pltpu.SMEM), vmem, hbm],
        out_specs=(hbm, hbm),
        scratch_shapes=[pltpu.VMEM((lanes, row_count, size), BF16)]
        + [pltpu.VMEM((groups * capacity, depth, size), BF16)] * DELIVER_STEPS
        + [
            dma,
            dma((lanes - 1,)),
            dma((lanes - 1,)),
            dma((DELIVER_STEPS,)),
            dma((DELIVER_STEPS, groups - 1)),
            dma((DELIVER_STEPS, groups - 1)),
            dma((DELIVER_STEPS,)),
            dma((DELIVER_STEPS, lanes - 1)),
            dma((DELIVER_STEPS, lanes - 1)),
        ],
        compiler_params=pltpu.CompilerParams(
            collective_id=0, has_side_effects=True, vmem_limit_bytes=20 << 20
        ),
        name="deliver",
    )(picks, turns, outgoing)


def gather_kernel(lanes, in_ref, out_ref, local, z_send, z_recv, p_send, p_recv, c_send, c_recv):
    row = lax.axis_index("row")
    me = lax.axis_index("star")
    depth = in_ref.shape[1] // GATHER_STEPS
    core = me + 1 - 2 * (me % 2)
    across = me + 2 - 4 * ((me // 2) % 2)
    along = me + 4 - 8 * ((me // 4) % 2)
    corner = across + 4 - 8 * ((me // 4) % 2)
    peers = [{"row": (row + d) % lanes} for d in range(1, lanes)]
    to_core, to_across, to_along = {"star": core}, {"star": across}, {"star": along}
    greet(peers + [to_core, to_across, to_along])
    half = lanes // 2
    started = []

    def start(copy):
        copy.start()
        started.append(copy)
        return copy

    def block(group, step, first=0, count=lanes):
        return out_ref.at[group, pl.ds(first, count), pl.ds(step * depth, depth)]

    own, exchanged = [], []
    for step in range(GATHER_STEPS):
        rows = pl.ds(step * depth, depth)
        copy = pltpu.make_async_copy(
            in_ref.at[row, rows], out_ref.at[me, row, rows], local.at[step]
        )
        copy.start()
        own.append(copy)
        exchanged.append(
            [
                start(
                    send(
                        in_ref.at[(row + d) % lanes, rows],
                        out_ref.at[me, row, rows],
                        z_send.at[step, d - 1],
                        z_recv.at[step, d - 1],
                        peers[d - 1],
                    )
                )
                for d in range(1, lanes)
            ]
        )

    def plane(step, way, part, peer):
        return start(send(part, part, p_send.at[step, way], p_recv.at[step, way], peer))

    def cores(step, way, part):
        return start(send(part, part, c_send.at[step, way], c_recv.at[step, way], to_core))

    sides, corners, twins = {}, {}, []
    for step in range(GATHER_STEPS + 2):
        if step < GATHER_STEPS:
            own[step].wait()
            for copy in exchanged[step]:
                copy.wait_recv()
            part = block(me, step)
            sides[step] = (
                plane(step, 0, part, to_across),
                plane(step, 1, part, to_along),
            )
            twins.append(cores(step, 0, part))
        last = step - 1
        if 0 <= last < GATHER_STEPS:
            sides[last][0].wait_recv()
            first = plane(last, 2, block(across, last, 0, half), to_along)
            twins.append(cores(last, 1, block(across, last)))
            sides[last][1].wait_recv()
            second = plane(last, 3, block(along, last, half, lanes - half), to_across)
            twins.append(cores(last, 2, block(along, last)))
            corners[last] = (first, second)
        last = step - 2
        if last >= 0:
            corners[last][0].wait_recv()
            corners[last][1].wait_recv()
            twins.append(cores(last, 3, block(corner, last)))
    for copy in twins:
        copy.wait_recv()
    for copy in started:
        copy.wait_send()


def gather_grads(path_grad, groups):
    lanes, row_count, size = path_grad.shape
    dma = pltpu.SemaphoreType.DMA
    return pl.pallas_call(
        functools.partial(gather_kernel, lanes),
        out_shape=jax.ShapeDtypeStruct((groups, lanes, row_count, size), path_grad.dtype),
        in_specs=[pl.BlockSpec(memory_space=pltpu.VMEM)],
        out_specs=pl.BlockSpec(memory_space=pl.ANY),
        scratch_shapes=[
            dma((GATHER_STEPS,)),
            dma((GATHER_STEPS, lanes - 1)),
            dma((GATHER_STEPS, lanes - 1)),
            dma((GATHER_STEPS, 4)),
            dma((GATHER_STEPS, 4)),
            dma((GATHER_STEPS, 4)),
            dma((GATHER_STEPS, 4)),
        ],
        compiler_params=pltpu.CompilerParams(
            collective_id=1, has_side_effects=True, vmem_limit_bytes=8 << 20
        ),
        name="gather_grads",
    )(path_grad)


def score_kernel(groups, lanes, in_ref, out_ref, z_send, z_recv, s_send, s_recv):
    row = lax.axis_index("row")
    me = lax.axis_index("star")
    row_peers = [{"row": (row + d) % lanes} for d in range(1, lanes)]
    star_peers = [{"star": (me + d) % groups} for d in range(1, groups)]
    greet(row_peers + star_peers)
    copies = [
        send(in_ref, out_ref.at[me, row], z_send.at[d], z_recv.at[d], row_peers[d])
        for d in range(lanes - 1)
    ]
    for copy in copies:
        copy.start()
    out_ref[me, row] = in_ref[...]
    for copy in copies:
        copy.wait()
    copies = [
        send(out_ref.at[me], out_ref.at[me], s_send.at[d], s_recv.at[d], star_peers[d])
        for d in range(groups - 1)
    ]
    for copy in copies:
        copy.start()
    for copy in copies:
        copy.wait()


def gather_scores(scores, groups, lanes):
    dma = pltpu.SemaphoreType.DMA
    vmem = pl.BlockSpec(memory_space=pltpu.VMEM)
    return pl.pallas_call(
        functools.partial(score_kernel, groups, lanes),
        out_shape=jax.ShapeDtypeStruct((groups, lanes) + scores.shape, scores.dtype),
        in_specs=[vmem],
        out_specs=vmem,
        scratch_shapes=[
            dma((lanes - 1,)),
            dma((lanes - 1,)),
            dma((groups - 1,)),
            dma((groups - 1,)),
        ],
        compiler_params=pltpu.CompilerParams(
            collective_id=2, has_side_effects=True, vmem_limit_bytes=8 << 20
        ),
        name="gather_scores",
    )(scores)


def star_devices(feature_maps, coef_table, star_counts, star_cells, star_bands, psf_cotangent):
    groups = lax.axis_size("star")
    lanes = lax.axis_size("row")
    my_group = lax.axis_index("star")
    my_lane = lax.axis_index("row")
    slot_count = psf_cotangent.shape[0]
    map_count, row_count, size = feature_maps.shape
    cell_count = coef_table.shape[0]
    share = map_count // groups
    group_ends = jnp.cumsum(star_counts)
    group_starts = group_ends - star_counts
    capacity = -(-slot_count // groups)
    targets = jnp.arange(groups, dtype=jnp.int32)
    my_start = table_pick(group_starts, my_group[None])
    first_slot = (targets - my_start) % groups
    lane_index = jnp.arange(capacity, dtype=jnp.int32)
    send_slot = (first_slot[:, None] + lane_index[None, :] * groups).reshape(-1)
    outgoing = jnp.take(
        psf_cotangent, jnp.minimum(send_slot, slot_count - 1), axis=0, mode="clip"
    )
    outgoing = outgoing.reshape((groups, capacity) + outgoing.shape[1:])

    total = groups * lanes
    order = jnp.arange(total, dtype=jnp.int32)
    rank = order // lanes + (order % lanes) * groups
    owner = jnp.sum((group_ends[None, :] <= rank[:, None]).astype(jnp.int32), axis=1)
    within = rank - table_pick(group_starts, owner)
    slot_index = owner * slot_count + within
    cell_ids = table_pick(star_cells.reshape(-1), slot_index)
    band_ids = table_pick(star_bands.reshape(-1), slot_index)
    cell_hot = cell_ids[:, None] == jnp.arange(cell_count, dtype=jnp.int32)[None, :]
    coef_rows = jnp.dot(
        cell_hot.astype(BF16), coef_table, preferred_element_type=F32
    ).astype(BF16)

    def mine(values):
        return lax.dynamic_slice_in_dim(values, my_group * lanes, lanes, 0)

    wavelength = 0.55 + 0.35 * band_ids.astype(F32) / (BANDS - 1)
    turns = phase_turns(mine(1.0 / wavelength), mine(coef_rows), feature_maps)
    picks = mine(owner) * capacity + mine(within) // groups
    turns, cotangent = deliver(picks, turns, outgoing)
    wave = wave_numbers(band_ids)
    my_wave = lax.dynamic_slice_in_dim(wave, my_group * lanes + my_lane, 1, 0)
    right, left = quarter_tables(size)
    path_grad = star_gradient(
        my_wave, turns.reshape(size, size), cotangent.reshape(size, size), right, left
    )
    path_grads = gather_grads(path_grad.reshape(lanes, row_count, size), groups)
    path_grads = path_grads.reshape(total, row_count, size)
    my_coefs = lax.dynamic_slice_in_dim(coef_rows.T, my_group * share, share, 0)
    map_grad, scores = map_sums(my_group, my_coefs, path_grads, feature_maps, share)
    scores = jnp.pad(scores, ((0, 0), (0, -total % 128)))
    scores = jnp.sum(gather_scores(scores, groups, lanes), axis=1)
    scores = scores.reshape(map_count, -1)[:, :total]
    coef_grad = lax.dot_general(
        cell_hot.astype(F32),
        scores * (1.0 / (8 * size)),
        (((0,), (1,)), ((), ())),
        precision=lax.Precision.HIGHEST,
    )
    return map_grad, coef_grad


def solution(mesh):
    placed = (P(None, "row", None), P(), P(), P(), P(), P("star", "row", None))
    fits = mesh.shape["row"] == LIVE_DEV and mesh.shape["star"] == PLANE_DEV
    device = star_devices if fits else per_device
    return jax.shard_map(
        device,
        mesh=mesh,
        in_specs=placed,
        out_specs=(P("star", "row", None), P()),
        check_vma=False,
    )
```

```python
import functools

import jax
import jax.numpy as jnp
import numpy as np
from jax import lax
from jax.experimental import pallas as pl
from jax.experimental.pallas import tpu as pltpu
from jax.sharding import PartitionSpec as P

BANDS = 8
LIVE_DEV = 4
PLANE_DEV = 8
RADIX = 4
ROWS_STEP = 16
F32 = jnp.float32
BF16 = jnp.bfloat16


def fourier_tables(pupil_size):
    index_row = jnp.arange(pupil_size, dtype=jnp.int32)
    products = index_row[:, None] * index_row[None, :] % pupil_size
    angles = 2.0 * jnp.pi / pupil_size * products.astype(jnp.float32)
    return (jnp.cos(angles).astype(jnp.bfloat16), (-jnp.sin(angles)).astype(jnp.bfloat16))


def aperture_rows(first_row, row_count, pupil_size):
    centre = 0.5 * (pupil_size - 1)
    row_pos = (first_row + jnp.arange(row_count, dtype=jnp.int32)).astype(jnp.float32) - centre
    col_pos = jnp.arange(pupil_size, dtype=jnp.int32).astype(jnp.float32) - centre
    radius = row_pos[:, None] * row_pos[:, None] + col_pos[None, :] * col_pos[None, :]
    return jnp.where(radius <= 0.25 * pupil_size * pupil_size, 1.0, 0.0).astype(jnp.float32)


def wave_numbers(band_ids):
    wavelength = 0.55 + 0.35 * band_ids.astype(jnp.float32) / (BANDS - 1)
    return 2.0 * jnp.pi / wavelength


def table_pick(values, indices):
    positions = jnp.arange(values.shape[0], dtype=jnp.int32)
    chosen = jnp.where(positions[None, :] == indices[:, None], values[None, :], 0)
    return jnp.sum(chosen, axis=1)


def per_device(feature_maps, coef_table, star_counts, star_cells, star_bands, psf_cotangent):
    groups = lax.axis_size("star")
    my_group = lax.axis_index("star")
    slot_count = psf_cotangent.shape[0]
    map_count, row_count, pupil_size = feature_maps.shape
    group_ends = jnp.cumsum(star_counts)
    group_starts = group_ends - star_counts
    flat_cells = star_cells.reshape(-1)
    flat_bands = star_bands.reshape(-1)
    cell_count = coef_table.shape[0]
    capacity = -(-slot_count // groups)
    targets = jnp.arange(groups, dtype=jnp.int32)
    lane_index = jnp.arange(capacity, dtype=jnp.int32)
    my_start = table_pick(group_starts, my_group[None])
    my_count = table_pick(star_counts, my_group[None])
    first_slot = (targets - my_start) % groups
    send_slot = (first_slot[:, None] + lane_index[None, :] * groups).reshape(-1)
    valid_mask = send_slot < my_count
    picked = jnp.take(psf_cotangent, jnp.minimum(send_slot, slot_count - 1), axis=0)
    outgoing = jnp.where(valid_mask[:, None, None], picked, jnp.zeros_like(picked))
    incoming = lax.all_to_all(outgoing, "star", split_axis=0, concat_axis=0, tiled=True)
    star_rank = my_group + jnp.arange(LIVE_DEV, dtype=jnp.int32) * groups
    owner_group = jnp.sum((group_ends[None, :] <= star_rank[:, None]).astype(jnp.int32), axis=1)
    within = star_rank - table_pick(group_starts, owner_group)
    live_mask = jnp.ones((LIVE_DEV,), dtype=bool)
    owner_group, within, live_mask = (owner_group, within, live_mask)
    cotangent = jnp.take(incoming, owner_group * capacity + within // groups, axis=0)
    slot_index = owner_group * slot_count + within
    cell_ids = table_pick(flat_cells, slot_index)
    band_ids = table_pick(flat_bands, slot_index)
    cell_hot = cell_ids[:, None] == jnp.arange(cell_count, dtype=jnp.int32)[None, :]
    coef_rows = jnp.dot(
        cell_hot.astype(jnp.bfloat16), coef_table, preferred_element_type=jnp.float32
    ).astype(jnp.bfloat16)
    flat_maps = feature_maps.reshape(map_count, row_count * pupil_size)
    path_error = jnp.dot(coef_rows, flat_maps, preferred_element_type=jnp.float32).reshape(
        -1, row_count, pupil_size
    )
    wave_number = wave_numbers(band_ids)
    phase_angle = wave_number[:, None, None] * path_error
    aperture = aperture_rows(lax.axis_index("row") * row_count, row_count, pupil_size)
    cos_phase = jnp.cos(phase_angle)
    sin_phase = jnp.sin(phase_angle)
    pupil_field = jnp.stack([aperture * cos_phase, aperture * sin_phase], 1).astype(jnp.bfloat16)
    cos_table, sin_table = fourier_tables(pupil_size)
    inverse = 1.0 / pupil_size
    along_cos = jnp.einsum(
        "sarc,cv->sarv", pupil_field, cos_table, preferred_element_type=jnp.float32
    )
    along_sin = jnp.einsum(
        "sarc,cv->sarv", pupil_field, sin_table, preferred_element_type=jnp.float32
    )
    column_field = jnp.stack(
        [along_cos[:, 0] - along_sin[:, 1], along_sin[:, 0] + along_cos[:, 1]], 1
    ).astype(jnp.bfloat16)
    pieces = lax.all_to_all(column_field, "row", split_axis=3, concat_axis=2, tiled=True)
    row_cos = jnp.einsum("sarv,ru->savu", pieces, cos_table, preferred_element_type=jnp.float32)
    row_sin = jnp.einsum("sarv,ru->savu", pieces, sin_table, preferred_element_type=jnp.float32)
    real_part = (row_cos[:, 0] - row_sin[:, 1]) * inverse
    imag_part = (row_sin[:, 0] + row_cos[:, 1]) * inverse
    focal_field = jnp.stack([real_part, imag_part], 1)
    weight = jnp.where(live_mask, 2.0, 0.0).astype(jnp.float32)[:, None, None, None]
    focal_grad = (weight * cotangent.astype(jnp.float32)[:, None] * focal_field).astype(
        jnp.bfloat16
    )
    back_cos = jnp.einsum(
        "savu,ur->savr", focal_grad, cos_table, preferred_element_type=jnp.float32
    )
    back_sin = jnp.einsum(
        "savu,ur->savr", focal_grad, sin_table, preferred_element_type=jnp.float32
    )
    spectrum_grad = jnp.stack(
        [(back_cos[:, 0] + back_sin[:, 1]) * inverse, (back_cos[:, 1] - back_sin[:, 0]) * inverse],
        1,
    ).astype(jnp.bfloat16)
    pieces = lax.all_to_all(spectrum_grad, "row", split_axis=3, concat_axis=2, tiled=True)
    col_cos = jnp.einsum("savr,vc->sarc", pieces, cos_table, preferred_element_type=jnp.float32)
    col_sin = jnp.einsum("savr,vc->sarc", pieces, sin_table, preferred_element_type=jnp.float32)
    pupil_grad = jnp.stack([col_cos[:, 0] + col_sin[:, 1], col_cos[:, 1] - col_sin[:, 0]], 1)
    phase_grad = aperture * (cos_phase * pupil_grad[:, 1] - sin_phase * pupil_grad[:, 0])
    path_grad = (
        (wave_number[:, None, None] * phase_grad)
        .astype(jnp.bfloat16)
        .reshape(-1, row_count * pupil_size)
    )
    map_scores = lax.dot_general(
        path_grad, flat_maps, (((1,), (1,)), ((), ())), preferred_element_type=jnp.float32
    )
    coef_part = lax.dot_general(
        cell_hot.astype(jnp.float32),
        map_scores * (1.0 / (8 * pupil_size)),
        (((0,), (0,)), ((), ())),
        precision=lax.Precision.HIGHEST,
    )
    coef_grad = lax.psum(coef_part, ("star", "row"))
    share = map_count // groups
    map_grad = lax.psum_scatter(
        lax.dot_general(
            coef_rows, path_grad, (((0,), (0,)), ((), ())), preferred_element_type=jnp.float32
        ),
        "star",
        scatter_dimension=0,
        tiled=True,
    )
    return (map_grad.reshape(share, row_count, pupil_size), coef_grad)


def quarter_tables(size):
    quarter = size // RADIX
    place = np.arange(quarter)[None, :, None]
    freq = RADIX * np.arange(quarter)[None, None, :] + np.arange(RADIX)[:, None, None]
    angle = 2.0 * np.pi / size * ((place * freq) % size)
    cosine, sine = np.cos(angle), -np.sin(angle)
    right = np.concatenate(
        [np.concatenate([cosine, sine], 2), np.concatenate([-sine, cosine], 2)], 1
    ).astype(np.float32)
    left = np.swapaxes(right, 1, 2)
    return jnp.asarray(right.astype(jnp.bfloat16)), jnp.asarray(left.astype(jnp.bfloat16))


def turn_cos_sin(turns):
    half = turns * np.float32(np.pi)
    square = half * half
    sine = jnp.full_like(square, -1.0 / 39916800.0)
    for term in (1.0 / 362880.0, -1.0 / 5040.0, 1.0 / 120.0, -1.0 / 6.0, 1.0):
        sine = sine * square + np.float32(term)
    sine = sine * half
    cosine = jnp.full_like(square, 1.0 / 479001600.0)
    for term in (-1.0 / 3628800.0, 1.0 / 40320.0, -1.0 / 720.0, 1.0 / 24.0, -0.5, 1.0):
        cosine = cosine * square + np.float32(term)
    return 1.0 - 2.0 * sine * sine, 2.0 * sine * cosine


def butterfly(real, imag, sign):
    sr, dr = real[0] + real[2], real[0] - real[2]
    si, di = imag[0] + imag[2], imag[0] - imag[2]
    tr, er = real[1] + real[3], real[1] - real[3]
    ti, ei = imag[1] + imag[3], imag[1] - imag[3]
    if sign < 0:
        er, ei = -er, -ei
    return (
        [sr + tr, dr - ei, sr - tr, dr + ei],
        [si + ti, di + er, si - ti, di - er],
    )


def phase_kernel(inverse_ref, weight_ref, maps_ref, out_ref):
    stars, rows, size = out_ref.shape
    maps = maps_ref[...].reshape(maps_ref.shape[0] * rows, size)
    path = jnp.dot(weight_ref[...], maps, preferred_element_type=F32)
    for star in range(stars):
        turns = path[star * rows : (star + 1) * rows] * inverse_ref[star]
        out_ref[star] = (turns - jnp.floor(turns + 0.5)).astype(BF16)


def phase_turns(inverse_wave, coef_rows, feature_maps):
    map_count, row_count, size = feature_maps.shape
    stars = coef_rows.shape[0]
    weights = spread_rows(coef_rows)
    return pl.pallas_call(
        phase_kernel,
        out_shape=jax.ShapeDtypeStruct((stars, row_count, size), BF16),
        grid=(row_count // ROWS_STEP,),
        in_specs=[
            pl.BlockSpec(memory_space=pltpu.SMEM),
            pl.BlockSpec(weights.shape, lambda i: (0, 0)),
            pl.BlockSpec((map_count, ROWS_STEP, size), lambda i: (0, i, 0)),
        ],
        out_specs=pl.BlockSpec((stars, ROWS_STEP, size), lambda i: (0, i, 0)),
        cost_estimate=pl.CostEstimate(
            flops=2 * stars * ROWS_STEP * map_count * row_count * size,
            bytes_accessed=2 * (map_count + stars) * row_count * size,
            transcendentals=0,
        ),
        compiler_params=pltpu.CompilerParams(vmem_limit_bytes=24 << 20),
        name="phase_turns",
    )(inverse_wave, weights, feature_maps)


def spread_rows(weights):
    eye = jnp.eye(ROWS_STEP, dtype=weights.dtype)
    outs, ins = weights.shape
    spread = weights[:, None, :, None] * eye[None, :, None, :]
    return spread.reshape(outs * ROWS_STEP, ins * ROWS_STEP)


def star_kernel(
    chunk, wave_ref, turns_ref, cot_ref, right_ref, left_ref, out_ref, pr, pi, yr, yi, ct, xr, xi
):
    size = turns_ref.shape[1]
    quarter = size // RADIX
    steps = size // chunk
    blocks = [slice(m * quarter, (m + 1) * quarter) for m in range(RADIX)]
    centre = 0.5 * (size - 1)
    scale = 1.0 / size

    def forward_columns(step, carry):
        rows = pl.ds(pl.multiple_of(step * chunk, chunk), chunk)
        cosine, sine = turn_cos_sin(turns_ref[rows, :].astype(F32))
        row_pos = (
            lax.broadcasted_iota(jnp.int32, (chunk, size), 0) + step * chunk
        ).astype(F32) - centre
        col_pos = lax.broadcasted_iota(jnp.int32, (chunk, size), 1).astype(F32) - centre
        inside = row_pos * row_pos + col_pos * col_pos <= 0.25 * size * size
        real = jnp.where(inside, cosine, 0.0)
        imag = jnp.where(inside, sine, 0.0)
        pr[rows, :] = real
        pi[rows, :] = imag
        mixed_real, mixed_imag = butterfly(
            [real[:, b] for b in blocks], [imag[:, b] for b in blocks], -1
        )
        for k in range(RADIX):
            both = jnp.concatenate([mixed_real[k].astype(BF16), mixed_imag[k].astype(BF16)], 1)
            made = jnp.dot(both, right_ref[k], preferred_element_type=F32).astype(BF16)
            yr[rows, blocks[k]] = made[:, :quarter]
            yi[rows, blocks[k]] = made[:, quarter:]
        return carry

    lax.fori_loop(0, steps, forward_columns, 0)

    def pick(k):
        j = lax.broadcasted_iota(jnp.int32, (quarter, size), 0)
        f = lax.broadcasted_iota(jnp.int32, (quarter, size), 1)
        return jnp.where(f == RADIX * j + k, 1.0, 0.0).astype(BF16)

    nt = (((1,), (1,)), ((), ()))
    for k in range(RADIX):
        part = lax.dot_general(
            pick(k), cot_ref[...], nt, preferred_element_type=F32
        ).astype(BF16)
        for m in range(RADIX):
            ct[blocks[k], blocks[m]] = lax.dot_general(
                part, pick(m), nt, preferred_element_type=F32
            )

    def focal(step, carry):
        cols = pl.ds(pl.multiple_of(step * quarter, quarter), quarter)
        mixed_real, mixed_imag = butterfly(
            [yr[b, cols].astype(F32) for b in blocks],
            [yi[b, cols].astype(F32) for b in blocks],
            -1,
        )
        back_real, back_imag = [], []
        for k in range(RADIX):
            both = jnp.concatenate([mixed_real[k].astype(BF16), mixed_imag[k].astype(BF16)], 0)
            field = jnp.dot(left_ref[k], both, preferred_element_type=F32)
            weight = ct[blocks[k], cols] * (2.0 * scale)
            grad = (field * jnp.concatenate([weight, weight], 0)).astype(BF16)
            back = jnp.dot(right_ref[k], grad, preferred_element_type=F32)
            back_real.append(back[:quarter])
            back_imag.append(back[quarter:])
        spec_real, spec_imag = butterfly(back_real, back_imag, 1)
        for m in range(RADIX):
            xr[blocks[m], cols] = (spec_real[m] * scale).astype(BF16)
            xi[blocks[m], cols] = (spec_imag[m] * scale).astype(BF16)
        return carry

    lax.fori_loop(0, RADIX, focal, 0)

    def inverse_columns(step, carry):
        rows = pl.ds(pl.multiple_of(step * chunk, chunk), chunk)
        part_real, part_imag = [], []
        for k in range(RADIX):
            both = jnp.concatenate([xr[rows, blocks[k]], xi[rows, blocks[k]]], 1)
            made = jnp.dot(both, left_ref[k], preferred_element_type=F32)
            part_real.append(made[:, :quarter])
            part_imag.append(made[:, quarter:])
        grad_real, grad_imag = butterfly(part_real, part_imag, 1)
        wave = wave_ref[0]
        for m in range(RADIX):
            grad = pr[rows, blocks[m]] * grad_imag[m] - pi[rows, blocks[m]] * grad_real[m]
            out_ref[rows, blocks[m]] = (wave * grad).astype(BF16)
        return carry

    lax.fori_loop(0, steps, inverse_columns, 0)


def star_gradient(wave, turns, cotangent, right, left):
    size = turns.shape[0]
    vmem = pl.BlockSpec(memory_space=pltpu.VMEM)
    square = (size, size)
    return pl.pallas_call(
        functools.partial(star_kernel, 128),
        out_shape=jax.ShapeDtypeStruct(square, BF16),
        in_specs=[pl.BlockSpec(memory_space=pltpu.SMEM), vmem, vmem, vmem, vmem],
        out_specs=vmem,
        scratch_shapes=[
            pltpu.VMEM(square, F32),
            pltpu.VMEM(square, F32),
            pltpu.VMEM(square, BF16),
            pltpu.VMEM(square, BF16),
            pltpu.VMEM(square, F32),
            pltpu.VMEM(square, BF16),
            pltpu.VMEM(square, BF16),
        ],
        compiler_params=pltpu.CompilerParams(vmem_limit_bytes=56 << 20),
        name="star_gradient",
    )(wave, turns, cotangent, right, left)


def maps_kernel(group_ref, weight_ref, grad_ref, maps_ref, out_ref, score_ref):
    share, rows, size = out_ref.shape
    grads = grad_ref[...].reshape(grad_ref.shape[0] * rows, size)
    maps = maps_ref[...].reshape(share * rows, size)
    total = jnp.dot(weight_ref[...], grads, preferred_element_type=F32)
    out_ref[...] = total.reshape(share, rows, size)

    @pl.when(pl.program_id(0) == 0)
    def _():
        score_ref[...] = jnp.zeros_like(score_ref)

    score_ref[...] += lax.dot_general(
        maps, grads, (((1,), (1,)), ((), ())), preferred_element_type=F32
    )


def map_sums(my_group, coef_rows, path_grads, feature_maps, share):
    stars, row_count, size = path_grads.shape
    weights = spread_rows(coef_rows)
    score_shape = (share * ROWS_STEP, stars * ROWS_STEP)
    map_grad, scores = pl.pallas_call(
        maps_kernel,
        out_shape=(
            jax.ShapeDtypeStruct((share, row_count, size), F32),
            jax.ShapeDtypeStruct(score_shape, F32),
        ),
        grid_spec=pltpu.PrefetchScalarGridSpec(
            num_scalar_prefetch=1,
            grid=(row_count // ROWS_STEP,),
            in_specs=[
                pl.BlockSpec(weights.shape, lambda i, g: (0, 0)),
                pl.BlockSpec((stars, ROWS_STEP, size), lambda i, g: (0, i, 0)),
                pl.BlockSpec((share, ROWS_STEP, size), lambda i, g: (g[0], i, 0)),
            ],
            out_specs=(
                pl.BlockSpec((share, ROWS_STEP, size), lambda i, g: (0, i, 0)),
                pl.BlockSpec(score_shape, lambda i, g: (0, 0)),
            ),
        ),
        compiler_params=pltpu.CompilerParams(vmem_limit_bytes=56 << 20),
        name="map_sums",
    )(my_group[None], weights, path_grads, feature_maps)
    eye = jnp.eye(ROWS_STEP, dtype=F32)
    scores = scores.reshape(share, ROWS_STEP, stars, ROWS_STEP)
    return map_grad, jnp.sum(scores * eye[None, :, None, :], axis=(1, 3))


GATHER_STEPS = 8


def greet(peers):
    barrier = pltpu.get_barrier_semaphore()
    for peer in peers:
        pl.semaphore_signal(barrier, inc=1, device_id=peer, device_id_type=pl.DeviceIdType.MESH)
    pl.semaphore_wait(barrier, len(peers))


def send(source, target, send_sem, recv_sem, peer):
    return pltpu.make_async_remote_copy(
        src_ref=source,
        dst_ref=target,
        send_sem=send_sem,
        recv_sem=recv_sem,
        device_id=peer,
        device_id_type=pl.DeviceIdType.MESH,
    )


DELIVER_STEPS = 4


def deliver_kernel(
    groups, lanes, pick_ref, turns_ref, cot_ref, turns_out, cot_out, stage, *scratch
):
    arrived, sems = scratch[:DELIVER_STEPS], scratch[DELIVER_STEPS:]
    t_local, t_send, t_recv, s_local, s_send, s_recv, z_local, z_send, z_recv = sems
    row = lax.axis_index("row")
    me = lax.axis_index("star")
    capacity = cot_ref.shape[1]
    depth = cot_ref.shape[2] // DELIVER_STEPS
    row_peers = [{"row": (row + d) % lanes} for d in range(1, lanes)]
    star_peers = [{"star": (me + d) % groups} for d in range(1, groups)]
    greet(row_peers + star_peers)
    turns = [
        send(
            turns_ref.at[(row + d) % lanes],
            turns_out.at[row],
            t_send.at[d - 1],
            t_recv.at[d - 1],
            row_peers[d - 1],
        )
        for d in range(1, lanes)
    ]
    turns.append(pltpu.make_async_copy(turns_ref.at[row], turns_out.at[row], t_local))
    for copy in turns:
        copy.start()
    steps = []
    for step in range(DELIVER_STEPS):
        rows = pl.ds(step * depth, depth)
        target = arrived[step].at[pl.ds(me * capacity, capacity)]
        copies = [
            send(
                cot_ref.at[(me + d) % groups, :, rows],
                target,
                s_send.at[step, d - 1],
                s_recv.at[step, d - 1],
                star_peers[d - 1],
            )
            for d in range(1, groups)
        ]
        copies.append(pltpu.make_async_copy(cot_ref.at[me, :, rows], target, s_local.at[step]))
        for copy in copies:
            copy.start()
        steps.append(copies)
    sent = []
    for step in range(DELIVER_STEPS):
        rows = pl.ds(step * depth, depth)
        for copy in steps[step]:
            copy.wait()
        for lane in range(lanes):
            stage[lane, rows] = arrived[step][pick_ref[lane]]
        copies = [
            send(
                stage.at[(row + d) % lanes, rows],
                cot_out.at[row, rows],
                z_send.at[step, d - 1],
                z_recv.at[step, d - 1],
                row_peers[d - 1],
            )
            for d in range(1, lanes)
        ]
        copies.append(
            pltpu.make_async_copy(stage.at[row, rows], cot_out.at[row, rows], z_local.at[step])
        )
        for copy in copies:
            copy.start()
        sent += copies
    for copy in turns + sent:
        copy.wait()


def deliver(picks, turns, outgoing):
    groups, capacity, row_count, size = outgoing.shape
    lanes = turns.shape[0]
    depth = row_count // DELIVER_STEPS
    dma = pltpu.SemaphoreType.DMA
    hbm = pl.BlockSpec(memory_space=pl.ANY)
    vmem = pl.BlockSpec(memory_space=pltpu.VMEM)
    shape = jax.ShapeDtypeStruct((lanes, row_count, size), BF16)
    return pl.pallas_call(
        functools.partial(deliver_kernel, groups, lanes),
        out_shape=(shape, shape),
        in_specs=[pl.BlockSpec(memory_space=pltpu.SMEM), vmem, hbm],
        out_specs=(hbm, hbm),
        scratch_shapes=[pltpu.VMEM((lanes, row_count, size), BF16)]
        + [pltpu.VMEM((groups * capacity, depth, size), BF16)] * DELIVER_STEPS
        + [
            dma,
            dma((lanes - 1,)),
            dma((lanes - 1,)),
            dma((DELIVER_STEPS,)),
            dma((DELIVER_STEPS, groups - 1)),
            dma((DELIVER_STEPS, groups - 1)),
            dma((DELIVER_STEPS,)),
            dma((DELIVER_STEPS, lanes - 1)),
            dma((DELIVER_STEPS, lanes - 1)),
        ],
        compiler_params=pltpu.CompilerParams(
            collective_id=0, has_side_effects=True, vmem_limit_bytes=56 << 20
        ),
        name="deliver",
    )(picks, turns, outgoing)


def gather_kernel(lanes, in_ref, out_ref, local, z_send, z_recv, p_send, p_recv, c_send, c_recv):
    row = lax.axis_index("row")
    me = lax.axis_index("star")
    depth = in_ref.shape[1] // GATHER_STEPS
    core = me + 1 - 2 * (me % 2)
    across = me + 2 - 4 * ((me // 2) % 2)
    along = me + 4 - 8 * ((me // 4) % 2)
    corner = across + 4 - 8 * ((me // 4) % 2)
    peers = [{"row": (row + d) % lanes} for d in range(1, lanes)]
    to_core, to_across, to_along = {"star": core}, {"star": across}, {"star": along}
    greet(peers + [to_core, to_across, to_along])
    half = lanes // 2
    started = []

    def start(copy):
        copy.start()
        started.append(copy)
        return copy

    def block(group, step, first=0, count=lanes):
        return out_ref.at[group, pl.ds(first, count), pl.ds(step * depth, depth)]

    own, exchanged = [], []
    for step in range(GATHER_STEPS):
        rows = pl.ds(step * depth, depth)
        copy = pltpu.make_async_copy(
            in_ref.at[row, rows], out_ref.at[me, row, rows], local.at[step]
        )
        copy.start()
        own.append(copy)
        exchanged.append(
            [
                start(
                    send(
                        in_ref.at[(row + d) % lanes, rows],
                        out_ref.at[me, row, rows],
                        z_send.at[step, d - 1],
                        z_recv.at[step, d - 1],
                        peers[d - 1],
                    )
                )
                for d in range(1, lanes)
            ]
        )

    def plane(step, way, part, peer):
        return start(send(part, part, p_send.at[step, way], p_recv.at[step, way], peer))

    def cores(step, way, part):
        return start(send(part, part, c_send.at[step, way], c_recv.at[step, way], to_core))

    sides, corners, twins = {}, {}, []
    for step in range(GATHER_STEPS + 2):
        if step < GATHER_STEPS:
            own[step].wait()
            for copy in exchanged[step]:
                copy.wait_recv()
            part = block(me, step)
            sides[step] = (
                plane(step, 0, part, to_across),
                plane(step, 1, part, to_along),
            )
            twins.append(cores(step, 0, part))
        last = step - 1
        if 0 <= last < GATHER_STEPS:
            sides[last][0].wait_recv()
            first = plane(last, 2, block(across, last, 0, half), to_along)
            twins.append(cores(last, 1, block(across, last)))
            sides[last][1].wait_recv()
            second = plane(last, 3, block(along, last, half, lanes - half), to_across)
            twins.append(cores(last, 2, block(along, last)))
            corners[last] = (first, second)
        last = step - 2
        if last >= 0:
            corners[last][0].wait_recv()
            corners[last][1].wait_recv()
            twins.append(cores(last, 3, block(corner, last)))
    for copy in twins:
        copy.wait_recv()
    for copy in started:
        copy.wait_send()


def gather_grads(path_grad, groups):
    lanes, row_count, size = path_grad.shape
    dma = pltpu.SemaphoreType.DMA
    return pl.pallas_call(
        functools.partial(gather_kernel, lanes),
        out_shape=jax.ShapeDtypeStruct((groups, lanes, row_count, size), path_grad.dtype),
        in_specs=[pl.BlockSpec(memory_space=pltpu.VMEM)],
        out_specs=pl.BlockSpec(memory_space=pl.ANY),
        scratch_shapes=[
            dma((GATHER_STEPS,)),
            dma((GATHER_STEPS, lanes - 1)),
            dma((GATHER_STEPS, lanes - 1)),
            dma((GATHER_STEPS, 4)),
            dma((GATHER_STEPS, 4)),
            dma((GATHER_STEPS, 4)),
            dma((GATHER_STEPS, 4)),
        ],
        compiler_params=pltpu.CompilerParams(
            collective_id=1, has_side_effects=True, vmem_limit_bytes=56 << 20
        ),
        name="gather_grads",
    )(path_grad)


def score_kernel(groups, lanes, in_ref, out_ref, z_send, z_recv, s_send, s_recv):
    row = lax.axis_index("row")
    me = lax.axis_index("star")
    row_peers = [{"row": (row + d) % lanes} for d in range(1, lanes)]
    star_peers = [{"star": (me + d) % groups} for d in range(1, groups)]
    greet(row_peers + star_peers)
    copies = [
        send(in_ref, out_ref.at[me, row], z_send.at[d], z_recv.at[d], row_peers[d])
        for d in range(lanes - 1)
    ]
    for copy in copies:
        copy.start()
    out_ref[me, row] = in_ref[...]
    for copy in copies:
        copy.wait()
    copies = [
        send(out_ref.at[me], out_ref.at[me], s_send.at[d], s_recv.at[d], star_peers[d])
        for d in range(groups - 1)
    ]
    for copy in copies:
        copy.start()
    for copy in copies:
        copy.wait()


def gather_scores(scores, groups, lanes):
    dma = pltpu.SemaphoreType.DMA
    vmem = pl.BlockSpec(memory_space=pltpu.VMEM)
    return pl.pallas_call(
        functools.partial(score_kernel, groups, lanes),
        out_shape=jax.ShapeDtypeStruct((groups, lanes) + scores.shape, scores.dtype),
        in_specs=[vmem],
        out_specs=vmem,
        scratch_shapes=[
            dma((lanes - 1,)),
            dma((lanes - 1,)),
            dma((groups - 1,)),
            dma((groups - 1,)),
        ],
        compiler_params=pltpu.CompilerParams(
            collective_id=2, has_side_effects=True, vmem_limit_bytes=8 << 20
        ),
        name="gather_scores",
    )(scores)


def star_devices(feature_maps, coef_table, star_counts, star_cells, star_bands, psf_cotangent):
    groups = lax.axis_size("star")
    lanes = lax.axis_size("row")
    my_group = lax.axis_index("star")
    my_lane = lax.axis_index("row")
    slot_count = psf_cotangent.shape[0]
    map_count, row_count, size = feature_maps.shape
    cell_count = coef_table.shape[0]
    share = map_count // groups
    group_ends = jnp.cumsum(star_counts)
    group_starts = group_ends - star_counts
    capacity = -(-slot_count // groups)
    targets = jnp.arange(groups, dtype=jnp.int32)
    my_start = table_pick(group_starts, my_group[None])
    first_slot = (targets - my_start) % groups
    lane_index = jnp.arange(capacity, dtype=jnp.int32)
    send_slot = (first_slot[:, None] + lane_index[None, :] * groups).reshape(-1)
    outgoing = jnp.take(
        psf_cotangent, jnp.minimum(send_slot, slot_count - 1), axis=0, mode="clip"
    )
    outgoing = outgoing.reshape((groups, capacity) + outgoing.shape[1:])

    total = groups * lanes
    order = jnp.arange(total, dtype=jnp.int32)
    rank = order // lanes + (order % lanes) * groups
    owner = jnp.sum((group_ends[None, :] <= rank[:, None]).astype(jnp.int32), axis=1)
    within = rank - table_pick(group_starts, owner)
    slot_index = owner * slot_count + within
    cell_ids = table_pick(star_cells.reshape(-1), slot_index)
    band_ids = table_pick(star_bands.reshape(-1), slot_index)
    cell_hot = cell_ids[:, None] == jnp.arange(cell_count, dtype=jnp.int32)[None, :]
    coef_rows = jnp.dot(
        cell_hot.astype(BF16), coef_table, preferred_element_type=F32
    ).astype(BF16)

    def mine(values):
        return lax.dynamic_slice_in_dim(values, my_group * lanes, lanes, 0)

    wavelength = 0.55 + 0.35 * band_ids.astype(F32) / (BANDS - 1)
    turns = phase_turns(mine(1.0 / wavelength), mine(coef_rows), feature_maps)
    picks = mine(owner) * capacity + mine(within) // groups
    turns, cotangent = deliver(picks, turns, outgoing)
    wave = wave_numbers(band_ids)
    my_wave = lax.dynamic_slice_in_dim(wave, my_group * lanes + my_lane, 1, 0)
    right, left = quarter_tables(size)
    path_grad = star_gradient(
        my_wave, turns.reshape(size, size), cotangent.reshape(size, size), right, left
    )
    path_grads = gather_grads(path_grad.reshape(lanes, row_count, size), groups)
    path_grads = path_grads.reshape(total, row_count, size)
    my_coefs = lax.dynamic_slice_in_dim(coef_rows.T, my_group * share, share, 0)
    map_grad, scores = map_sums(my_group, my_coefs, path_grads, feature_maps, share)
    scores = jnp.pad(scores, ((0, 0), (0, -total % 128)))
    scores = jnp.sum(gather_scores(scores, groups, lanes), axis=1)
    scores = scores.reshape(map_count, -1)[:, :total]
    coef_grad = lax.dot_general(
        cell_hot.astype(F32),
        scores * (1.0 / (8 * size)),
        (((0,), (1,)), ((), ())),
        precision=lax.Precision.HIGHEST,
    )
    return map_grad, coef_grad


def solution(mesh):
    placed = (P(None, "row", None), P(), P(), P(), P(), P("star", "row", None))
    fits = mesh.shape["row"] == LIVE_DEV and mesh.shape["star"] == PLANE_DEV
    device = star_devices if fits else per_device
    return jax.shard_map(
        device,
        mesh=mesh,
        in_specs=placed,
        out_specs=(P("star", "row", None), P()),
        check_vma=False,
    )
```
